768 devices in a mesh: row: 96 (over z, y_lo, core), col: 8 (over x, y_hi).
Axes of the slice: x: 4, y: 8 (y_hi: 2, y_lo: 4; y = y_hi * 4 + y_lo), z: 12, core: 2. Of those that a mesh axis runs over, the one named last changes fastest.
Arguments:
- specimen: float32 [2, 12288, 1024], P(None, 'row', 'col'), may hold values from -4 to 4
- probe_mode_stack: float32 [4, 2, 256, 256], replicated, may hold values from -4 to 4
- measured: float32 [96, 8, 1, 256, 256], P('row', 'col'), may hold values from 0.3 to 3
- centers: int32 [96, 8, 2, 2], P('row', 'col'), may hold values from 1 to 127
- frame_counts: int32 [96, 8], P('row', 'col'), may hold values from 0 to 2, as said below
- helper_cols: int32 [96, 8, 2], P('row', 'col'), may hold values from 0 to 7, as said below
Outputs:
- gradient: float32 [2, 12288, 1024], P(None, 'row', 'col')
The draws below stay inside these ranges and needn't reach their ends.
Inputs may be any that keep to these rules, and one draw needn't show every extreme that they name: `frame_counts`: in every row of tiles the counts sum to 1 times the number of tiles in the row, and some tile of every row holds 2 frames. `helper_cols`: among a tile's live slots the helper columns are distinct; in every row of tiles each column is named by exactly one live slot; slots past a tile's count hold arbitrary columns.
All inputs are finite; a program needn't handle non-finite values.
Results may differ from the reference program's by a relative error of at most 0.007.
Values may be sent and summed in bfloat16 or wider, within the bound.
A program may use at most 32 MiB of HBM per device.

```python
import math
import jax
import jax.numpy as jnp
from jax import lax

FRAME_PIXELS = 256
MODES = 4
CAP = 2
HELPER_FRAMES = 1
TILE = 128
TILE_ROWS = 96
TILE_COLUMNS = 8
OBJ_R = 12288
OBJ_C = 1024


def plan_rows(key):
    folded = jax.random.fold_in(key, 4242)
    row_keys = jax.random.split(folded, TILE_ROWS)

    def one_row(row_key):
        key_order, key_extra, key_offset, key_helpers = jax.random.split(row_key, 4)
        ranking = jnp.argsort(jax.random.permutation(key_order, TILE_COLUMNS)).astype(jnp.int32)
        extra_move = jax.random.randint(key_extra, (), 0, 2, dtype=jnp.int32)
        counts_row = 1 + (ranking == 0).astype(jnp.int32) - (ranking == 1).astype(jnp.int32)
        counts_row = counts_row + extra_move * ((ranking == 2).astype(jnp.int32) - (ranking == 3).astype(jnp.int32))
        starts = jnp.cumsum(counts_row) - counts_row
        offset = jax.random.randint(key_offset, (), 0, TILE_COLUMNS, dtype=jnp.int32)
        helpers = jax.random.permutation(key_helpers, TILE_COLUMNS).astype(jnp.int32)
        slot_range = jnp.arange(CAP, dtype=jnp.int32)
        targets_row = helpers[(starts[:, None] + slot_range[None, :] + offset) % TILE_COLUMNS]
        return (counts_row.astype(jnp.int32), targets_row.astype(jnp.int32))
    return jax.vmap(one_row)(row_keys)


def draw_frame_counts(key, part):
    return plan_rows(key)[0]


def draw_helper_cols(key, part):
    return plan_rows(key)[1]


def place_ends(result, stream_key, low, largest):
    longest = result.shape.index(max(result.shape))
    spots = []
    for shift in (0, 1):
        where = [jax.random.randint(jax.random.fold_in(stream_key, axis), (), 0, length) for axis, length in enumerate(result.shape)]
        where[longest] = (where[longest] + shift) % result.shape[longest]
        spots.append(tuple(where))
    return result.at[spots[0]].set(low).at[spots[1]].set(largest)


def block_scale(rng, shape, cuts, smallest, high):
    def one(dim, parts):
        steps = jax.random.uniform(jax.random.fold_in(jax.random.fold_in(rng, 6), dim), (parts,), jnp.float32, smallest / len(cuts), high / len(cuts))
        return jnp.repeat(jnp.exp(steps), shape[dim] // parts).reshape((-1,) + (1,) * (len(shape) - dim - 1))

    loudness = one(*cuts[0])
    for cut in cuts[1:]:
        loudness = loudness * one(*cut)
    return loudness


def gaussian(own_key, dims, deviation, limit, cuts=(), kind=jnp.bfloat16):
    array = jax.random.normal(own_key, dims, jnp.float32) * deviation
    if len(cuts) > 0:
        array = block_scale(own_key, dims, cuts, -0.22, 0.18) * array
    return jnp.clip(array, min=-limit, max=limit).astype(kind)


def setup_inputs(seed: int = 0) -> dict:
    streams_of = jax.random.split(jax.random.key(seed), 7)
    return {
        "specimen": gaussian(streams_of[0], (2, OBJ_R, OBJ_C), 0.5, 4.0, ((1, 96), (2, 8)), jnp.float32),
        "probe_mode_stack": gaussian(streams_of[1], (MODES, 2, FRAME_PIXELS, FRAME_PIXELS), 0.5, 4.0, (), jnp.float32),
        "measured": jnp.clip(jnp.exp(math.log(3.0) - 2.3025851 * jax.random.uniform(streams_of[2], (TILE_ROWS, TILE_COLUMNS, HELPER_FRAMES, FRAME_PIXELS, FRAME_PIXELS), jnp.float32) ** block_scale(streams_of[2], (TILE_ROWS, TILE_COLUMNS, HELPER_FRAMES, FRAME_PIXELS, FRAME_PIXELS), ((0, 96), (1, 8)), -0.2, 0.2)), 0.3, 3.0),
        "centers": place_ends(jax.random.randint(streams_of[3], (TILE_ROWS, TILE_COLUMNS, CAP, 2), 1, TILE), jax.random.fold_in(streams_of[3], 1), 1, TILE - 1).astype(jnp.int32),
        "frame_counts": draw_frame_counts(jax.random.fold_in(streams_of[6], 71), 0),
        "helper_cols": draw_helper_cols(jax.random.fold_in(streams_of[6], 71), 0),
    }


def dft_tables(extent):
    steps_idx = jnp.arange(extent, dtype=jnp.int32)
    product = steps_idx[:, None] * steps_idx[None, :] % extent
    angles = product.astype(jnp.float32) * (2.0 * math.pi / extent)
    scaling = 1.0 / math.sqrt(extent)
    return ((jnp.cos(angles) * scaling).astype(jnp.bfloat16), (-jnp.sin(angles) * scaling).astype(jnp.bfloat16))

def widen_exact(values):
    return lax.optimization_barrier(values).astype(jnp.float32)

def right_apply(operand, fourier_real_table, fourier_imaginary_table, conj_sign):
    extent = fourier_real_table.shape[0]
    joined = widen_exact(jnp.concatenate([fourier_real_table, fourier_imaginary_table], axis=1))
    products = jnp.einsum('bxy,yv->bxv', widen_exact(operand), joined, precision=lax.Precision.HIGHEST)
    real_part = products[:, :extent, :extent] - conj_sign * products[:, extent:, extent:]
    imag_part = products[:, extent:, :extent] + conj_sign * products[:, :extent, extent:]
    return jnp.concatenate([real_part, imag_part], axis=1)

def left_apply(operand, fourier_real_table, fourier_imaginary_table, conj_sign):
    upper_rows = jnp.concatenate([fourier_real_table, -conj_sign * fourier_imaginary_table], axis=1)
    lower_rows = jnp.concatenate([conj_sign * fourier_imaginary_table, fourier_real_table], axis=1)
    mixer_matrix = widen_exact(jnp.concatenate([upper_rows, lower_rows], axis=0))
    return jnp.einsum('uv,bvc->buc', mixer_matrix, widen_exact(operand), precision=lax.Precision.HIGHEST)

def per_frame_gradients(object_patches, probe_mode_stack, measured, fourier_real_table, fourier_imaginary_table):
    helper_slot_count = object_patches.shape[0]
    extent = object_patches.shape[2]
    mode_count = probe_mode_stack.shape[0]
    wide_patch = widen_exact(object_patches)
    patch_re = wide_patch[:, None, :extent]
    patch_im = wide_patch[:, None, extent:]
    probe_re = probe_mode_stack[None, :, 0]
    probe_im = probe_mode_stack[None, :, 1]
    exit_wave = jnp.concatenate([probe_re * patch_re - probe_im * patch_im, probe_re * patch_im + probe_im * patch_re], axis=2)
    exit_wave = exit_wave.astype(jnp.bfloat16).reshape(helper_slot_count * mode_count, 2 * extent, extent)
    half_wave = right_apply(exit_wave, fourier_real_table, fourier_imaginary_table, 1.0).astype(jnp.bfloat16)
    far_field = left_apply(half_wave, fourier_real_table, fourier_imaginary_table, 1.0).reshape(helper_slot_count, mode_count, 2 * extent, extent)
    far_re = far_field[:, :, :extent]
    far_im = far_field[:, :, extent:]
    intensity = lax.optimization_barrier(jnp.sum(far_re * far_re + far_im * far_im, axis=1))
    factor = 1.0 - measured / jnp.sqrt(jnp.maximum(intensity, 0.25))
    doubled = jnp.concatenate([factor, factor], axis=1)[:, None]
    corrected = (far_field * doubled).astype(jnp.bfloat16).reshape(helper_slot_count * mode_count, 2 * extent, extent)
    back_half = right_apply(corrected, fourier_real_table, fourier_imaginary_table, -1.0).astype(jnp.bfloat16)
    inverse = left_apply(back_half, fourier_real_table, fourier_imaginary_table, -1.0).reshape(helper_slot_count, mode_count, 2 * extent, extent)
    chi_re = inverse[:, :, :extent]
    chi_im = inverse[:, :, extent:]
    grad_re = lax.optimization_barrier(jnp.sum(probe_re * chi_re + probe_im * chi_im, axis=1))
    grad_im = lax.optimization_barrier(jnp.sum(probe_re * chi_im - probe_im * chi_re, axis=1))
    return jnp.concatenate([grad_re, grad_im], axis=1).astype(jnp.bfloat16)

def reference(specimen, probe_mode_stack, measured, centers, frame_counts, helper_cols):
    half_size = FRAME_PIXELS // 2
    fourier_real_table, fourier_imaginary_table = dft_tables(FRAME_PIXELS)
    slots_range = jnp.arange(CAP, dtype=jnp.int32)
    is_live = slots_range[None, None, :] < frame_counts[:, :, None]
    helper_range = jnp.arange(TILE_COLUMNS, dtype=jnp.int32)
    hit_table = is_live[:, :, None, :] & (helper_cols[:, :, None, :] == helper_range[None, None, :, None])
    has_frame = jnp.any(hit_table, axis=3).astype(jnp.int32)
    before = (jnp.cumsum(has_frame, axis=1) - has_frame).astype(jnp.int32)
    select = has_frame[..., None] * (before[..., None] == jnp.arange(HELPER_FRAMES, dtype=jnp.int32)[None, None, None, :]).astype(jnp.int32)
    src_col = lax.optimization_barrier(jnp.sum(select * helper_range[None, :, None, None], axis=1)).astype(jnp.int32)
    frame_slot = lax.optimization_barrier(jnp.sum(hit_table.astype(jnp.int32) * slots_range[None, None, None, :], axis=3)).astype(jnp.int32)
    src_slot = lax.optimization_barrier(jnp.sum(select * frame_slot[..., None], axis=1)).astype(jnp.int32)
    row_range = jnp.arange(TILE_ROWS, dtype=jnp.int32)[:, None, None]
    picked = centers[row_range, src_col, src_slot]
    first_row = (row_range * TILE + picked[..., 0]).reshape(TILE_ROWS * TILE_COLUMNS, HELPER_FRAMES).astype(jnp.int32)
    first_column = (src_col * TILE + picked[..., 1]).reshape(TILE_ROWS * TILE_COLUMNS, HELPER_FRAMES).astype(jnp.int32)
    padded = jnp.pad(specimen, ((0, 0), (half_size, half_size), (half_size, half_size)))
    flat_measurements = measured.reshape(TILE_ROWS * TILE_COLUMNS, HELPER_FRAMES, FRAME_PIXELS, FRAME_PIXELS)

    def process_helper_frame(summed_gradient, input_arrays):
        row_positions, column_positions, current_measurements = input_arrays
        pieces = []
        for slot_idx in range(HELPER_FRAMES):
            corner = (jnp.int32(0), row_positions[slot_idx], column_positions[slot_idx])
            pieces.append(lax.dynamic_slice(padded, corner, (2, FRAME_PIXELS, FRAME_PIXELS)).reshape(2 * FRAME_PIXELS, FRAME_PIXELS))
        object_patches = jnp.stack(pieces).astype(jnp.bfloat16)
        patch_gradients = per_frame_gradients(object_patches, probe_mode_stack, current_measurements, fourier_real_table, fourier_imaginary_table)
        for slot_idx in range(HELPER_FRAMES):
            corner = (jnp.int32(0), row_positions[slot_idx], column_positions[slot_idx])
            current = lax.dynamic_slice(summed_gradient, corner, (2, FRAME_PIXELS, FRAME_PIXELS))
            added = current + widen_exact(patch_gradients[slot_idx]).reshape(2, FRAME_PIXELS, FRAME_PIXELS)
            summed_gradient = lax.dynamic_update_slice(summed_gradient, added, corner)
        return (summed_gradient, None)
    summed_gradient = jnp.zeros(padded.shape, jnp.float32)
    summed_gradient, ignored_value = lax.scan(process_helper_frame, summed_gradient, (first_row, first_column, flat_measurements))
    return summed_gradient[:, half_size:half_size + OBJ_R, half_size:half_size + OBJ_C]
```

```python
import functools
import math

import jax
import jax.numpy as jnp
import numpy as np
from jax import lax
from jax.experimental import pallas as pl
from jax.experimental.pallas import tpu as pltpu
from jax.sharding import PartitionSpec as P

MESH = pl.DeviceIdType.MESH
F32 = jnp.float32
BF16 = jnp.bfloat16


def dft_blocks(extent):
    idx = np.arange(extent)
    angles = (idx[:, None] * idx[None, :] % extent) * (2.0 * math.pi / extent)
    scale = 1.0 / math.sqrt(extent)
    re, im = np.cos(angles) * scale, -np.sin(angles) * scale
    return np.block([[re, im], [-im, re]])


def dot(a, b):
    return jnp.dot(a, b, preferred_element_type=F32)


def kernel(
    n_r,
    n_c,
    centers,
    counts,
    helpers,
    spec,
    measured,
    probe_hbm,
    fwd_hbm,
    bwd_hbm,
    out,
    probe,
    fwd,
    bwd,
    meta,
    nb,
    meas,
    rows_buf,
    cols_buf,
    far,
    zbuf,
    g_own,
    g_on,
    g_off,
    g_sum,
    r_on_buf,
    r_buf,
    local_sem,
    meta_sem,
    halo_send,
    halo_recv,
    meas_send,
    meas_recv,
    grad_send,
    grad_recv,
):
    t = spec.shape[1]
    n = probe.shape[-1]
    modes = probe.shape[0]
    r, c = lax.axis_index("row"), lax.axis_index("col")
    odd_r, odd_c = lax.rem(r, 2), lax.rem(c, 2)
    r_on = r + 1 - 2 * odd_r
    r_off = lax.rem(r - 1 + 2 * odd_r + n_r, n_r)
    c_x = c + 1 - 2 * odd_c
    c_give = lax.rem(c - 2 + 4 * odd_c + n_c, n_c)
    c_take = lax.rem(c + 2 - 4 * odd_c + n_c, n_c)
    peers = [lax.rem(c + 2 * k, n_c) for k in range(1, n_c // 2)]

    barrier = pltpu.get_barrier_semaphore()
    partners = [(r_on, c), (r_off, c), (r, c_x), (r_off, c_x), (r_off, c_give), (r_off, c_take)]
    partners += [(r, p) for p in peers]
    for partner in partners:
        pl.semaphore_signal(barrier, inc=1, device_id=partner, device_id_type=MESH)

    loads = [
        pltpu.make_async_copy(src, dst, local_sem.at[i])
        for i, (src, dst) in enumerate([(probe_hbm, probe), (fwd_hbm, fwd), (bwd_hbm, bwd)])
    ]
    for load in loads:
        load.start()

    nb[0] = jnp.concatenate([spec[0], spec[1]], axis=1).astype(BF16)
    values = [centers[0], centers[1], centers[2], centers[3], helpers[0], helpers[1], counts[0]]
    which = lax.broadcasted_iota(jnp.int32, (8, 128), 0)
    block = jnp.zeros((8, 128), jnp.int32)
    for i, value in enumerate(values):
        block = jnp.where(which == i, value, block)
    meta[0] = block
    meas[c] = measured[...].astype(BF16)

    pl.semaphore_wait(barrier, len(partners))

    def remote(src, dst, send, recv, device):
        return pltpu.make_async_remote_copy(
            src_ref=src,
            dst_ref=dst,
            send_sem=send,
            recv_sem=recv,
            device_id=device,
            device_id_type=MESH,
        )

    def halo(src, dst, device):
        return remote(nb.at[src], nb.at[dst], halo_send.at[dst], halo_recv.at[dst], device)

    to_x = halo(0, 1, (r, c_x))
    to_off_x = halo(0, 7, (r_off, c_x))
    to_far = halo(0, 2, (r, c_give))
    to_off_far = halo(0, 8, (r_off, c_give))
    to_off = halo(0, 6, (r_off, c))
    to_on = halo(0, 3, (r_on, c))
    meta_copy = remote(meta.at[0], meta.at[1], meta_sem.at[0], meta_sem.at[1], (r, c_x))
    first = [meta_copy, to_x, to_off_x, to_off_far, to_far, to_off, to_on]
    for copy in first:
        copy.start()
    meas_x = remote(meas.at[c], meas.at[c], meas_send.at[0], meas_recv.at[0], (r, c_x))
    meas_x.start()
    meas_own = [
        remote(meas.at[c], meas.at[c], meas_send.at[k + 1], meas_recv.at[k + 1], (r, p))
        for k, p in enumerate(peers)
    ]
    for copy in meas_own:
        copy.start()

    to_x.wait_recv()
    fwd_x = halo(1, 4, (r_on, c))
    fwd_x.start()
    to_far.wait_recv()
    fwd_far = halo(2, 5, (r_on, c))
    fwd_far.start()

    meta_copy.wait_recv()
    info = meta[1]
    cr = [info[0:1, 0:1], info[2:3, 0:1]]
    cc = [info[1:2, 0:1], info[3:4, 0:1]]
    hc = [info[4:5, 0:1], info[5:6, 0:1]]
    live = [info[6:7, 0:1] > s for s in range(2)]

    nowhere = -4 * n
    row_on, row_off = 2 * t * (1 - odd_r), 2 * t * odd_r
    row_off = jnp.where((r == 0) | (r == n_r - 1), nowhere, row_off)
    col_own, col_far = 2 * t * odd_c, 2 * t * (1 - odd_c)
    col_far = jnp.where((c == 1) | (c == n_c - 2), nowhere, col_far)

    def place(idx, first_, second, third):
        role = idx // t
        base = jnp.where(role == 0, first_, jnp.where(role == 1, second, third))
        return base + idx - role * t

    def one_hot(shape, axis, roles, start):
        role_idx = lax.broadcasted_iota(jnp.int32, shape, axis)
        pix = lax.broadcasted_iota(jnp.int32, shape, 1 - axis)
        return jnp.where(place(role_idx, *roles) == pix + start, 1.0, 0.0).astype(BF16)

    row_roles = (t, row_on, row_off)
    col_roles = (col_own, t, col_far)
    row_at = [jnp.where(live[s], cr[s], 8 * n) for s in range(2)]

    for copy in (to_off, to_off_x, to_off_far, to_on, fwd_x, fwd_far):
        copy.wait_recv()
    for load in loads:
        load.wait()

    tiles = [jnp.concatenate([nb[j], nb[3 + j], nb[6 + j]], axis=0) for j in range(3)]

    for s in range(2):
        pick = one_hot((n, 3 * t), 1, row_roles, row_at[s])
        cut = [dot(pick, tiles[j]).astype(BF16) for j in range(3)]
        strip = jnp.concatenate(
            [
                jnp.concatenate([x[:, :t] for x in cut], axis=1),
                jnp.concatenate([x[:, t:] for x in cut], axis=1),
            ],
            axis=0,
        )
        patch = dot(strip, one_hot((3 * t, n), 0, col_roles, cc[s]))
        re, im = patch[:n], patch[n:]
        for k in range(modes):
            p_re, p_im = probe[k, 0], probe[k, 1]
            rows_buf[k * n : (k + 1) * n, :n] = (p_re * re - p_im * im).astype(BF16)
            rows_buf[k * n : (k + 1) * n, n:] = (p_re * im + p_im * re).astype(BF16)
        for k in range(modes):
            half = dot(rows_buf[k * n : (k + 1) * n], fwd[...]).astype(BF16)
            cols_buf[:n, k * n : (k + 1) * n] = half[:, :n]
            cols_buf[n:, k * n : (k + 1) * n] = half[:, n:]
        far[s] = dot(bwd[...], cols_buf[...])

    meas_x.wait_recv()
    meas_fwd = [
        remote(
            meas.at[c_x],
            meas.at[c_x],
            meas_send.at[n_c // 2 + k],
            meas_recv.at[n_c // 2 + k],
            (r, p),
        )
        for k, p in enumerate(peers)
    ]
    for copy in meas_fwd:
        copy.start()
    for copy in meas_own + meas_fwd:
        copy.wait_recv()

    for s in range(2):
        intensity = jnp.zeros((n, n), F32)
        for k in range(modes):
            f_re = far[s, :n, k * n : (k + 1) * n]
            f_im = far[s, n:, k * n : (k + 1) * n]
            intensity = intensity + (f_re * f_re + f_im * f_im)
        amp = jnp.zeros((n, n), F32)
        for h in range(n_c):
            amp = amp + jnp.where(hc[s] == h, meas[h].astype(F32), 0.0)
        factor = 1.0 - amp * lax.rsqrt(jnp.maximum(intensity, 0.25))
        for k in range(modes):
            for part in range(2):
                f = far[s, part * n : (part + 1) * n, k * n : (k + 1) * n]
                rows_buf[k * n : (k + 1) * n, part * n : (part + 1) * n] = (f * factor).astype(BF16)
        for k in range(modes):
            back = dot(rows_buf[k * n : (k + 1) * n], bwd[...]).astype(BF16)
            cols_buf[:n, k * n : (k + 1) * n] = back[:, :n]
            cols_buf[n:, k * n : (k + 1) * n] = back[:, n:]
        far[s] = dot(fwd[...], cols_buf[...])
        g_re = jnp.zeros((n, n), F32)
        g_im = jnp.zeros((n, n), F32)
        for k in range(modes):
            p_re, p_im = probe[k, 0], probe[k, 1]
            x_re = far[s, :n, k * n : (k + 1) * n]
            x_im = far[s, n:, k * n : (k + 1) * n]
            g_re = g_re + (p_re * x_re + p_im * x_im)
            g_im = g_im + (p_re * x_im - p_im * x_re)
        grad = jnp.concatenate([g_re, g_im], axis=0).astype(BF16)
        wide = dot(grad, one_hot((n, 3 * t), 1, col_roles, cc[s])).astype(BF16)
        for j in range(3):
            zbuf[j, s * n : (s + 1) * n, :t] = wide[:n, j * t : (j + 1) * t]
            zbuf[j, s * n : (s + 1) * n, t:] = wide[n:, j * t : (j + 1) * t]

    spread = jnp.concatenate(
        [one_hot((3 * t, n), 0, row_roles, row_at[s]) for s in range(2)], axis=1
    )
    for j in range(3):
        total = dot(spread, zbuf[j])
        g_own[j] = total[:t]
        g_on[j] = total[t : 2 * t].astype(BF16)
        g_off[j] = total[2 * t :].astype(BF16)

    def grad_copy(src, dst, i, device):
        return remote(src, dst, grad_send.at[i], grad_recv.at[i], device)

    on_copy = grad_copy(g_on, r_on_buf, 0, (r_on, c))
    on_copy.start()
    off_x = grad_copy(g_off.at[1], r_buf.at[0], 1, (r_off, c_x))
    off_far = grad_copy(g_off.at[2], r_buf.at[1], 2, (r_off, c_take))
    off_own = grad_copy(g_off.at[0], r_buf.at[2], 3, (r_off, c))
    for copy in (off_x, off_far, off_own):
        copy.start()
    on_copy.wait_recv()
    for j in (1, 2):
        g_sum[j - 1] = (g_own[j] + r_on_buf[j].astype(F32)).astype(BF16)
    sum_x = grad_copy(g_sum.at[0], r_buf.at[3], 4, (r, c_x))
    sum_far = grad_copy(g_sum.at[1], r_buf.at[4], 5, (r, c_take))
    sum_x.start()
    sum_far.start()
    mine = g_own[0] + r_on_buf[0].astype(F32)
    grads = (off_x, off_far, off_own, sum_x, sum_far)
    for copy in grads:
        copy.wait_recv()
    for i in range(5):
        mine = mine + r_buf[i].astype(F32)
    out[0] = mine[:, :t]
    out[1] = mine[:, t:]
    for copy in first + [meas_x, fwd_x, fwd_far, on_copy] + meas_own + meas_fwd + list(grads):
        copy.wait_send()


def per_device(n_r, n_c, tables, specimen, probe, measured, centers, counts, helpers):
    t = specimen.shape[1]
    modes, _, n, _ = probe.shape
    fwd, bwd = tables
    vmem = pl.BlockSpec(memory_space=pltpu.VMEM)
    smem = pl.BlockSpec(memory_space=pltpu.SMEM)
    hbm = pl.BlockSpec(memory_space=pl.ANY)
    dma = pltpu.SemaphoreType.DMA
    return pl.pallas_call(
        functools.partial(kernel, n_r, n_c),
        out_shape=jax.ShapeDtypeStruct(specimen.shape, F32),
        in_specs=[smem, smem, smem, vmem, vmem, hbm, hbm, hbm],
        out_specs=vmem,
        scratch_shapes=[
            pltpu.VMEM(probe.shape, F32),
            pltpu.VMEM((2 * n, 2 * n), BF16),
            pltpu.VMEM((2 * n, 2 * n), BF16),
            pltpu.VMEM((2, 8, 128), jnp.int32),
            pltpu.VMEM((9, t, 2 * t), BF16),
            pltpu.VMEM((n_c, n, n), BF16),
            pltpu.VMEM((modes * n, 2 * n), BF16),
            pltpu.VMEM((2 * n, modes * n), BF16),
            pltpu.VMEM((2, 2 * n, modes * n), F32),
            pltpu.VMEM((3, 2 * n, 2 * t), BF16),
            pltpu.VMEM((3, t, 2 * t), F32),
            pltpu.VMEM((3, t, 2 * t), BF16),
            pltpu.VMEM((3, t, 2 * t), BF16),
            pltpu.VMEM((2, t, 2 * t), BF16),
            pltpu.VMEM((3, t, 2 * t), BF16),
            pltpu.VMEM((5, t, 2 * t), BF16),
            dma((3,)),
            dma((2,)),
            dma((9,)),
            dma((9,)),
            dma((n_c,)),
            dma((n_c,)),
            dma((6,)),
            dma((6,)),
        ],
        compiler_params=pltpu.CompilerParams(
            collective_id=0, has_side_effects=True, vmem_limit_bytes=56 * 1024 * 1024
        ),
    )(
        centers.reshape(4),
        counts.reshape(1),
        helpers.reshape(2),
        specimen,
        measured.reshape(n, n),
        probe,
        fwd,
        bwd,
    )


def solution(mesh):
    n_r, n_c = mesh.shape["row"], mesh.shape["col"]

    def program(specimen, probe, measured, centers, counts, helpers):
        base = dft_blocks(probe.shape[-1])
        tables = (jnp.asarray(base, BF16), jnp.asarray(base.T, BF16))
        return jax.shard_map(
            functools.partial(per_device, n_r, n_c, tables),
            mesh=mesh,
            in_specs=(
                P(None, "row", "col"),
                P(),
                P("row", "col", None, None, None),
                P("row", "col", None, None),
                P("row", "col"),
                P("row", "col", None),
            ),
            out_specs=P(None, "row", "col"),
            check_vma=False,
        )(specimen, probe, measured, centers, counts, helpers)

    return program
```

```python
import functools
import math

import jax
import jax.numpy as jnp
import numpy as np
from jax import lax
from jax.experimental import pallas as pl
from jax.experimental.pallas import tpu as pltpu
from jax.sharding import PartitionSpec as P

MESH = pl.DeviceIdType.MESH
F32 = jnp.float32
BF16 = jnp.bfloat16
CHUNKS = 4


def dft_blocks(extent):
    idx = np.arange(extent)
    angles = (idx[:, None] * idx[None, :] % extent) * (2.0 * math.pi / extent)
    scale = 1.0 / math.sqrt(extent)
    re, im = np.cos(angles) * scale, -np.sin(angles) * scale
    return np.block([[re, im], [-im, re]])


def dot(a, b):
    return jnp.dot(a, b, preferred_element_type=F32)


def kernel(
    n_r,
    n_c,
    centers,
    counts,
    helpers,
    spec,
    measured,
    probe_hbm,
    fwd_hbm,
    bwd_hbm,
    out,
    probe,
    fwd,
    bwd,
    meta,
    nb,
    meas,
    rows_buf,
    cols_buf,
    far,
    zbuf,
    g_own,
    g_on,
    g_off,
    g_sum,
    r_on_buf,
    r_buf,
    local_sem,
    meta_sem,
    halo_send,
    halo_recv,
    meas_send,
    meas_recv,
    grad_send,
    grad_recv,
):
    t = spec.shape[1]
    n = probe.shape[-1]
    modes = probe.shape[0]
    r, c = lax.axis_index("row"), lax.axis_index("col")
    odd_r, odd_c = lax.rem(r, 2), lax.rem(c, 2)
    r_on = r + 1 - 2 * odd_r
    r_off = lax.rem(r - 1 + 2 * odd_r + n_r, n_r)
    inside = (r > 0) & (r < n_r - 1)
    c_x = c + 1 - 2 * odd_c
    c_give = lax.rem(c - 2 + 4 * odd_c + n_c, n_c)
    c_take = lax.rem(c + 2 - 4 * odd_c + n_c, n_c)
    peers = [lax.rem(c + 2 * k, n_c) for k in range(1, n_c // 2)]

    barrier = pltpu.get_barrier_semaphore()
    near = [(r_on, c), (r, c_x)] + [(r, p) for p in peers]
    across = [(r_off, c), (r_off, c_x), (r_off, c_give), (r_off, c_take)]

    def greet(partners):
        for partner in partners:
            pl.semaphore_signal(barrier, inc=1, device_id=partner, device_id_type=MESH)

    greet(near)
    pl.when(inside)(lambda: greet(across))

    loads = [
        pltpu.make_async_copy(src, dst, local_sem.at[i])
        for i, (src, dst) in enumerate([(probe_hbm, probe), (fwd_hbm, fwd), (bwd_hbm, bwd)])
    ]
    for load in loads:
        load.start()

    nb[0] = jnp.concatenate([spec[0], spec[1]], axis=1).astype(BF16)
    values = [centers[0, 0, i, j] for i in range(2) for j in range(2)]
    values += [helpers[0, 0, 0], helpers[0, 0, 1], counts[...]]
    which = lax.broadcasted_iota(jnp.int32, (8, 128), 0)
    block = jnp.zeros((8, 128), jnp.int32)
    for i, value in enumerate(values):
        block = jnp.where(which == i, value, block)
    meta[0] = block
    meas[c] = measured[...].astype(BF16).reshape(meas.shape[1:])

    @pl.when(jnp.logical_not(inside))
    def _():
        nb[6:9] = jnp.zeros((3, t, 2 * t), BF16)
        r_buf[0:3] = jnp.zeros((3, t, 2 * t), BF16)

    pl.semaphore_wait(barrier, len(near) + jnp.where(inside, len(across), 0))

    def remote(src, dst, send, recv, device):
        return pltpu.make_async_remote_copy(
            src_ref=src,
            dst_ref=dst,
            send_sem=send,
            recv_sem=recv,
            device_id=device,
            device_id_type=MESH,
        )

    def halo(src, dst, device):
        return remote(nb.at[src], nb.at[dst], halo_send.at[dst], halo_recv.at[dst], device)

    to_x = halo(0, 1, (r, c_x))
    to_off_x = halo(0, 7, (r_off, c_x))
    to_far = halo(0, 2, (r, c_give))
    to_off_far = halo(0, 8, (r_off, c_give))
    to_off = halo(0, 6, (r_off, c))
    to_on = halo(0, 3, (r_on, c))
    meta_copy = remote(meta.at[0], meta.at[1], meta_sem.at[0], meta_sem.at[1], (r, c_x))
    first = [meta_copy, to_x, to_far, to_on]
    across_copies = [to_off_x, to_off_far, to_off]

    def start(copies):
        for copy in copies:
            copy.start()

    def wait_recv(copies):
        for copy in copies:
            copy.wait_recv()

    def wait_send(copies):
        for copy in copies:
            copy.wait_send()

    start(first[:2])
    pl.when(inside)(lambda: start(across_copies))
    start(first[2:])

    chunks = meas.shape[1]
    sides = n_c // 2 - 1

    def meas_copy(src, sem, device):
        return remote(src, src, meas_send.at[sem], meas_recv.at[sem], device)

    meas_x = [meas_copy(meas.at[c, q], q, (r, c_x)) for q in range(chunks)]
    meas_own = [meas_copy(meas.at[c], chunks + k, (r, p)) for k, p in enumerate(peers)]
    meas_fwd = [
        [
            meas_copy(meas.at[c_x, q], chunks + sides * (q + 1) + k, (r, p))
            for k, p in enumerate(peers)
        ]
        for q in range(chunks)
    ]
    start(meas_x)
    start(meas_own)

    def pass_on(some):
        for q in some:
            meas_x[q].wait_recv()
            start(meas_fwd[q])

    to_x.wait_recv()
    fwd_x = halo(1, 4, (r_on, c))
    fwd_x.start()
    to_far.wait_recv()
    fwd_far = halo(2, 5, (r_on, c))
    fwd_far.start()

    meta_copy.wait_recv()
    info = meta[1]
    cr = [info[0:1, 0:1], info[2:3, 0:1]]
    cc = [info[1:2, 0:1], info[3:4, 0:1]]
    hc = [info[4:5, 0:1], info[5:6, 0:1]]
    live = [info[6:7, 0:1] > s for s in range(2)]

    nowhere = -4 * n
    row_on, row_off = 2 * t * (1 - odd_r), 2 * t * odd_r
    row_off = jnp.where((r == 0) | (r == n_r - 1), nowhere, row_off)
    col_own, col_far = 2 * t * odd_c, 2 * t * (1 - odd_c)
    col_far = jnp.where((c == 1) | (c == n_c - 2), nowhere, col_far)

    def place(idx, first_, second, third):
        role = idx // t
        base = jnp.where(role == 0, first_, jnp.where(role == 1, second, third))
        return base + idx - role * t

    def one_hot(shape, axis, roles, start):
        role_idx = lax.broadcasted_iota(jnp.int32, shape, axis)
        pix = lax.broadcasted_iota(jnp.int32, shape, 1 - axis)
        return jnp.where(place(role_idx, *roles) == pix + start, 1.0, 0.0).astype(BF16)

    row_roles = (t, row_on, row_off)
    col_roles = (col_own, t, col_far)
    row_at = [jnp.where(live[s], cr[s], 8 * n) for s in range(2)]

    pl.when(inside)(lambda: wait_recv(across_copies))
    wait_recv([to_on, fwd_x, fwd_far])
    for load in loads:
        load.wait()

    tiles = [jnp.concatenate([nb[j], nb[3 + j], nb[6 + j]], axis=0) for j in range(3)]

    for s in range(2):
        pick = one_hot((n, 3 * t), 1, row_roles, row_at[s])
        cut = [dot(pick, tiles[j]).astype(BF16) for j in range(3)]
        strip = jnp.concatenate(
            [
                jnp.concatenate([x[:, :t] for x in cut], axis=1),
                jnp.concatenate([x[:, t:] for x in cut], axis=1),
            ],
            axis=0,
        )
        patch = dot(strip, one_hot((3 * t, n), 0, col_roles, cc[s]))
        re, im = patch[:n], patch[n:]
        for k in range(modes):
            p_re, p_im = probe[k, 0], probe[k, 1]
            rows_buf[k * n : (k + 1) * n, :n] = (p_re * re - p_im * im).astype(BF16)
            rows_buf[k * n : (k + 1) * n, n:] = (p_re * im + p_im * re).astype(BF16)
        for k in range(modes):
            half = dot(rows_buf[k * n : (k + 1) * n], fwd[...]).astype(BF16)
            cols_buf[:n, k * n : (k + 1) * n] = half[:, :n]
            cols_buf[n:, k * n : (k + 1) * n] = half[:, n:]
        far[s] = dot(bwd[...], cols_buf[...])
        pass_on(range(s * chunks // 2, (s + 1) * chunks // 2))

    wait_recv(meas_own + sum(meas_fwd, []))

    for s in range(2):
        intensity = jnp.zeros((n, n), F32)
        for k in range(modes):
            f_re = far[s, :n, k * n : (k + 1) * n]
            f_im = far[s, n:, k * n : (k + 1) * n]
            intensity = intensity + (f_re * f_re + f_im * f_im)
        amp = jnp.zeros((n, n), F32)
        for h in range(n_c):
            amp = amp + jnp.where(hc[s] == h, meas[h].reshape(n, n).astype(F32), 0.0)
        factor = 1.0 - amp * lax.rsqrt(jnp.maximum(intensity, 0.25))
        for k in range(modes):
            for part in range(2):
                f = far[s, part * n : (part + 1) * n, k * n : (k + 1) * n]
                rows_buf[k * n : (k + 1) * n, part * n : (part + 1) * n] = (f * factor).astype(BF16)
        for k in range(modes):
            back = dot(rows_buf[k * n : (k + 1) * n], bwd[...]).astype(BF16)
            cols_buf[:n, k * n : (k + 1) * n] = back[:, :n]
            cols_buf[n:, k * n : (k + 1) * n] = back[:, n:]
        far[s] = dot(fwd[...], cols_buf[...])
        g_re = jnp.zeros((n, n), F32)
        g_im = jnp.zeros((n, n), F32)
        for k in range(modes):
            p_re, p_im = probe[k, 0], probe[k, 1]
            x_re = far[s, :n, k * n : (k + 1) * n]
            x_im = far[s, n:, k * n : (k + 1) * n]
            g_re = g_re + (p_re * x_re + p_im * x_im)
            g_im = g_im + (p_re * x_im - p_im * x_re)
        grad = jnp.concatenate([g_re, g_im], axis=0).astype(BF16)
        wide = dot(grad, one_hot((n, 3 * t), 1, col_roles, cc[s])).astype(BF16)
        for j in range(3):
            zbuf[j, s * n : (s + 1) * n, :t] = wide[:n, j * t : (j + 1) * t]
            zbuf[j, s * n : (s + 1) * n, t:] = wide[n:, j * t : (j + 1) * t]

    spread = jnp.concatenate(
        [one_hot((3 * t, n), 0, row_roles, row_at[s]) for s in range(2)], axis=1
    )
    for j in range(3):
        total = dot(spread, zbuf[j])
        g_own[j] = total[:t]
        g_on[j] = total[t : 2 * t].astype(BF16)
        g_off[j] = total[2 * t :].astype(BF16)

    def grad_copy(src, dst, i, device):
        return remote(src, dst, grad_send.at[i], grad_recv.at[i], device)

    on_copy = grad_copy(g_on, r_on_buf, 0, (r_on, c))
    on_copy.start()
    off_x = grad_copy(g_off.at[1], r_buf.at[0], 1, (r_off, c_x))
    off_far = grad_copy(g_off.at[2], r_buf.at[1], 2, (r_off, c_take))
    off_own = grad_copy(g_off.at[0], r_buf.at[2], 3, (r_off, c))
    across_grads = [off_x, off_far, off_own]
    pl.when(inside)(lambda: start(across_grads))
    on_copy.wait_recv()
    for j in (1, 2):
        g_sum[j - 1] = (g_own[j] + r_on_buf[j].astype(F32)).astype(BF16)
    sum_x = grad_copy(g_sum.at[0], r_buf.at[3], 4, (r, c_x))
    sum_far = grad_copy(g_sum.at[1], r_buf.at[4], 5, (r, c_take))
    sum_x.start()
    sum_far.start()
    mine = g_own[0] + r_on_buf[0].astype(F32)
    pl.when(inside)(lambda: wait_recv(across_grads))
    wait_recv([sum_x, sum_far])
    for i in range(5):
        mine = mine + r_buf[i].astype(F32)
    out[0] = mine[:, :t]
    out[1] = mine[:, t:]
    wait_send(first + meas_x + [fwd_x, fwd_far, on_copy, sum_x, sum_far])
    wait_send(meas_own + sum(meas_fwd, []))
    pl.when(inside)(lambda: wait_send(across_copies + across_grads))


def per_device(n_r, n_c, tables, specimen, probe, measured, centers, counts, helpers):
    t = specimen.shape[1]
    modes, _, n, _ = probe.shape
    fwd, bwd = tables
    vmem = pl.BlockSpec(memory_space=pltpu.VMEM)
    smem = pl.BlockSpec(memory_space=pltpu.SMEM)
    hbm = pl.BlockSpec(memory_space=pl.ANY)
    dma = pltpu.SemaphoreType.DMA
    return pl.pallas_call(
        functools.partial(kernel, n_r, n_c),
        out_shape=jax.ShapeDtypeStruct(specimen.shape, F32),
        in_specs=[smem, vmem, smem, vmem, vmem, hbm, hbm, hbm],
        out_specs=vmem,
        scratch_shapes=[
            pltpu.VMEM(probe.shape, F32),
            pltpu.VMEM((2 * n, 2 * n), BF16),
            pltpu.VMEM((2 * n, 2 * n), BF16),
            pltpu.VMEM((2, 8, 128), jnp.int32),
            pltpu.VMEM((9, t, 2 * t), BF16),
            pltpu.VMEM((n_c, CHUNKS, n // CHUNKS, n), BF16),
            pltpu.VMEM((modes * n, 2 * n), BF16),
            pltpu.VMEM((2 * n, modes * n), BF16),
            pltpu.VMEM((2, 2 * n, modes * n), F32),
            pltpu.VMEM((3, 2 * n, 2 * t), BF16),
            pltpu.VMEM((3, t, 2 * t), F32),
            pltpu.VMEM((3, t, 2 * t), BF16),
            pltpu.VMEM((3, t, 2 * t), BF16),
            pltpu.VMEM((2, t, 2 * t), BF16),
            pltpu.VMEM((3, t, 2 * t), BF16),
            pltpu.VMEM((5, t, 2 * t), BF16),
            dma((3,)),
            dma((2,)),
            dma((9,)),
            dma((9,)),
            dma((CHUNKS + (CHUNKS + 1) * (n_c // 2 - 1),)),
            dma((CHUNKS + (CHUNKS + 1) * (n_c // 2 - 1),)),
            dma((6,)),
            dma((6,)),
        ],
        compiler_params=pltpu.CompilerParams(
            collective_id=0, has_side_effects=True, vmem_limit_bytes=56 * 1024 * 1024
        ),
    )(
        centers,
        counts,
        helpers,
        specimen,
        measured.reshape(n, n),
        probe,
        fwd,
        bwd,
    )


def solution(mesh):
    n_r, n_c = mesh.shape["row"], mesh.shape["col"]

    def program(specimen, probe, measured, centers, counts, helpers):
        base = dft_blocks(probe.shape[-1])
        tables = (jnp.asarray(base, BF16), jnp.asarray(base.T, BF16))
        return jax.shard_map(
            functools.partial(per_device, n_r, n_c, tables),
            mesh=mesh,
            in_specs=(
                P(None, "row", "col"),
                P(),
                P("row", "col", None, None, None),
                P("row", "col", None, None),
                P("row", "col"),
                P("row", "col", None),
            ),
            out_specs=P(None, "row", "col"),
            check_vma=False,
        )(specimen, probe, measured, centers, counts, helpers)

    return program
```

```python
import functools
import math

import jax
import jax.numpy as jnp
import numpy as np
from jax import lax
from jax.experimental import pallas as pl
from jax.experimental.pallas import tpu as pltpu
from jax.sharding import PartitionSpec as P

MESH = pl.DeviceIdType.MESH
F32 = jnp.float32
BF16 = jnp.bfloat16
CHUNKS = 4


def dft_blocks(extent):
    idx = np.arange(extent)
    angles = (idx[:, None] * idx[None, :] % extent) * (2.0 * math.pi / extent)
    scale = 1.0 / math.sqrt(extent)
    re, im = np.cos(angles) * scale, -np.sin(angles) * scale
    return np.block([[re, im], [-im, re]])


def dot(a, b):
    return jnp.dot(a, b, preferred_element_type=F32)


def kernel(
    n_r,
    n_c,
    centers,
    counts,
    helpers,
    spec_hbm,
    measured_hbm,
    probe_hbm,
    fwd_hbm,
    bwd_hbm,
    out,
    spec,
    measured,
    probe,
    fwd,
    bwd,
    meta,
    nb,
    meas,
    rows_buf,
    cols_buf,
    far,
    zbuf,
    g_own,
    g_on,
    g_off,
    g_sum,
    r_on_buf,
    r_buf,
    local_sem,
    meta_sem,
    halo_send,
    halo_recv,
    meas_send,
    meas_recv,
    grad_send,
    grad_recv,
):
    t = spec.shape[1]
    n = probe.shape[-1]
    modes = probe.shape[0]
    r, c = lax.axis_index("row"), lax.axis_index("col")
    odd_r, odd_c = lax.rem(r, 2), lax.rem(c, 2)
    r_on = r + 1 - 2 * odd_r
    r_off = lax.rem(r - 1 + 2 * odd_r + n_r, n_r)
    inside = (r > 0) & (r < n_r - 1)
    c_x = c + 1 - 2 * odd_c
    c_give = lax.rem(c - 2 + 4 * odd_c + n_c, n_c)
    c_take = lax.rem(c + 2 - 4 * odd_c + n_c, n_c)
    peers = [lax.rem(c + 2 * k, n_c) for k in range(1, n_c // 2)]

    barrier = pltpu.get_barrier_semaphore()
    near = [(r_on, c), (r, c_x)] + [(r, p) for p in peers]
    across = [(r_off, c), (r_off, c_x), (r_off, c_give), (r_off, c_take)]

    def greet(partners):
        for partner in partners:
            pl.semaphore_signal(barrier, inc=1, device_id=partner, device_id_type=MESH)

    greet(near)
    pl.when(inside)(lambda: greet(across))

    loads = [
        pltpu.make_async_copy(src, dst, local_sem.at[i])
        for i, (src, dst) in enumerate(
            [
                (spec_hbm, spec),
                (measured_hbm, measured),
                (probe_hbm, probe),
                (fwd_hbm, fwd),
                (bwd_hbm, bwd),
            ]
        )
    ]
    for load in loads:
        load.start()

    loads[0].wait()
    nb[0] = jnp.concatenate([spec[0], spec[1]], axis=1).astype(BF16)
    values = [centers[0, 0, i, j] for i in range(2) for j in range(2)]
    values += [helpers[0, 0, 0], helpers[0, 0, 1], counts[...]]
    which = lax.broadcasted_iota(jnp.int32, (8, 128), 0)
    block = jnp.zeros((8, 128), jnp.int32)
    for i, value in enumerate(values):
        block = jnp.where(which == i, value, block)
    meta[0] = block
    loads[1].wait()
    meas[c] = measured[...].astype(BF16).reshape(meas.shape[1:])

    @pl.when(jnp.logical_not(inside))
    def _():
        nb[6:9] = jnp.zeros((3, t, 2 * t), BF16)
        r_buf[0:3] = jnp.zeros((3, t, 2 * t), BF16)

    pl.semaphore_wait(barrier, len(near) + jnp.where(inside, len(across), 0))

    def remote(src, dst, send, recv, device):
        return pltpu.make_async_remote_copy(
            src_ref=src,
            dst_ref=dst,
            send_sem=send,
            recv_sem=recv,
            device_id=device,
            device_id_type=MESH,
        )

    def halo(src, dst, device):
        return remote(nb.at[src], nb.at[dst], halo_send.at[dst], halo_recv.at[dst], device)

    to_x = halo(0, 1, (r, c_x))
    to_off_x = halo(0, 7, (r_off, c_x))
    to_far = halo(0, 2, (r, c_give))
    to_off_far = halo(0, 8, (r_off, c_give))
    to_off = halo(0, 6, (r_off, c))
    to_on = halo(0, 3, (r_on, c))
    meta_copy = remote(meta.at[0], meta.at[1], meta_sem.at[0], meta_sem.at[1], (r, c_x))
    first = [meta_copy, to_x, to_far, to_on]
    across_copies = [to_off_x, to_off_far, to_off]

    def start(copies):
        for copy in copies:
            copy.start()

    def wait_recv(copies):
        for copy in copies:
            copy.wait_recv()

    def wait_send(copies):
        for copy in copies:
            copy.wait_send()

    start(first[:2])
    pl.when(inside)(lambda: start(across_copies))
    start(first[2:])

    chunks = meas.shape[1]
    sides = n_c // 2 - 1

    def meas_copy(src, sem, device):
        return remote(src, src, meas_send.at[sem], meas_recv.at[sem], device)

    meas_x = [meas_copy(meas.at[c, q], q, (r, c_x)) for q in range(chunks)]
    meas_own = [meas_copy(meas.at[c], chunks + k, (r, p)) for k, p in enumerate(peers)]
    meas_fwd = [
        [
            meas_copy(meas.at[c_x, q], chunks + sides * (q + 1) + k, (r, p))
            for k, p in enumerate(peers)
        ]
        for q in range(chunks)
    ]
    start(meas_x)
    start(meas_own)

    def pass_on(some):
        for q in some:
            meas_x[q].wait_recv()
            start(meas_fwd[q])

    to_x.wait_recv()
    fwd_x = halo(1, 4, (r_on, c))
    fwd_x.start()
    to_far.wait_recv()
    fwd_far = halo(2, 5, (r_on, c))
    fwd_far.start()

    meta_copy.wait_recv()
    info = meta[1]
    cr = [info[0:1, 0:1], info[2:3, 0:1]]
    cc = [info[1:2, 0:1], info[3:4, 0:1]]
    hc = [info[4:5, 0:1], info[5:6, 0:1]]
    live = [info[6:7, 0:1] > s for s in range(2)]

    nowhere = -4 * n
    row_on, row_off = 2 * t * (1 - odd_r), 2 * t * odd_r
    row_off = jnp.where((r == 0) | (r == n_r - 1), nowhere, row_off)
    col_own, col_far = 2 * t * odd_c, 2 * t * (1 - odd_c)
    col_far = jnp.where((c == 1) | (c == n_c - 2), nowhere, col_far)

    def place(idx, first_, second, third):
        role = idx // t
        base = jnp.where(role == 0, first_, jnp.where(role == 1, second, third))
        return base + idx - role * t

    def one_hot(shape, axis, roles, start):
        role_idx = lax.broadcasted_iota(jnp.int32, shape, axis)
        pix = lax.broadcasted_iota(jnp.int32, shape, 1 - axis)
        return jnp.where(place(role_idx, *roles) == pix + start, 1.0, 0.0).astype(BF16)

    row_roles = (t, row_on, row_off)
    col_roles = (col_own, t, col_far)
    row_at = [jnp.where(live[s], cr[s], 8 * n) for s in range(2)]

    pl.when(inside)(lambda: wait_recv(across_copies))
    wait_recv([to_on, fwd_x, fwd_far])
    for load in loads[2:]:
        load.wait()

    tiles = [jnp.concatenate([nb[j], nb[3 + j], nb[6 + j]], axis=0) for j in range(3)]

    for s in range(2):
        pick = one_hot((n, 3 * t), 1, row_roles, row_at[s])
        cut = [dot(pick, tiles[j]).astype(BF16) for j in range(3)]
        strip = jnp.concatenate(
            [
                jnp.concatenate([x[:, :t] for x in cut], axis=1),
                jnp.concatenate([x[:, t:] for x in cut], axis=1),
            ],
            axis=0,
        )
        patch = dot(strip, one_hot((3 * t, n), 0, col_roles, cc[s]))
        re, im = patch[:n], patch[n:]
        for k in range(modes):
            p_re, p_im = probe[k, 0], probe[k, 1]
            rows_buf[s, k * n : (k + 1) * n, :n] = (p_re * re - p_im * im).astype(BF16)
            rows_buf[s, k * n : (k + 1) * n, n:] = (p_re * im + p_im * re).astype(BF16)
        for k in range(modes):
            half = dot(rows_buf[s, k * n : (k + 1) * n], fwd[...]).astype(BF16)
            cols_buf[s, :n, k * n : (k + 1) * n] = half[:, :n]
            cols_buf[s, n:, k * n : (k + 1) * n] = half[:, n:]
        far[s] = dot(bwd[...], cols_buf[s])
        pass_on(range(s * chunks // 2, (s + 1) * chunks // 2))

    w = n // chunks
    wait_recv(meas_own)
    for q in range(chunks):
        wait_recv(meas_fwd[q])
        lo, block = q * w, modes * w
        for s in range(2):
            intensity = jnp.zeros((w, n), F32)
            for k in range(modes):
                f_re = far[s, lo : lo + w, k * n : (k + 1) * n]
                f_im = far[s, n + lo : n + lo + w, k * n : (k + 1) * n]
                intensity = intensity + (f_re * f_re + f_im * f_im)
            amp = jnp.zeros((w, n), F32)
            for h in range(n_c):
                amp = amp + jnp.where(hc[s] == h, meas[h, q].astype(F32), 0.0)
            factor = 1.0 - amp * lax.rsqrt(jnp.maximum(intensity, 0.25))
            for k in range(modes):
                at = q * block + k * w
                for part in range(2):
                    row = part * n + lo
                    f = far[s, row : row + w, k * n : (k + 1) * n]
                    rows_buf[s, at : at + w, part * n : (part + 1) * n] = (f * factor).astype(BF16)
            back = dot(rows_buf[s, q * block : (q + 1) * block], bwd[...]).astype(BF16)
            for k in range(modes):
                for part in range(2):
                    row = part * n + lo
                    cols_buf[s, row : row + w, k * n : (k + 1) * n] = back[
                        k * w : (k + 1) * w, part * n : (part + 1) * n
                    ]

    for s in range(2):
        far[s] = dot(fwd[...], cols_buf[s])
        g_re = jnp.zeros((n, n), F32)
        g_im = jnp.zeros((n, n), F32)
        for k in range(modes):
            p_re, p_im = probe[k, 0], probe[k, 1]
            x_re = far[s, :n, k * n : (k + 1) * n]
            x_im = far[s, n:, k * n : (k + 1) * n]
            g_re = g_re + (p_re * x_re + p_im * x_im)
            g_im = g_im + (p_re * x_im - p_im * x_re)
        grad = jnp.concatenate([g_re, g_im], axis=0).astype(BF16)
        wide = dot(grad, one_hot((n, 3 * t), 1, col_roles, cc[s])).astype(BF16)
        for j in range(3):
            zbuf[j, s * n : (s + 1) * n, :t] = wide[:n, j * t : (j + 1) * t]
            zbuf[j, s * n : (s + 1) * n, t:] = wide[n:, j * t : (j + 1) * t]

    spread = jnp.concatenate(
        [one_hot((3 * t, n), 0, row_roles, row_at[s]) for s in range(2)], axis=1
    )

    def grad_copy(src, dst, i, device):
        return remote(src, dst, grad_send.at[i], grad_recv.at[i], device)

    order = (1, 2, 0)
    on_copies = [grad_copy(g_on.at[j], r_on_buf.at[j], 5 + j, (r_on, c)) for j in range(3)]
    for j in order:
        g_on[j] = dot(spread[t : 2 * t], zbuf[j]).astype(BF16)
        on_copies[j].start()
    for j in order:
        g_off[j] = dot(spread[2 * t :], zbuf[j]).astype(BF16)
    off_x = grad_copy(g_off.at[1], r_buf.at[0], 0, (r_off, c_x))
    off_far = grad_copy(g_off.at[2], r_buf.at[1], 1, (r_off, c_take))
    off_own = grad_copy(g_off.at[0], r_buf.at[2], 2, (r_off, c))
    across_grads = [off_x, off_far, off_own]
    pl.when(inside)(lambda: start(across_grads))
    for j in order:
        g_own[j] = dot(spread[:t], zbuf[j])
    sum_x = grad_copy(g_sum.at[0], r_buf.at[3], 3, (r, c_x))
    sum_far = grad_copy(g_sum.at[1], r_buf.at[4], 4, (r, c_take))
    for j, copy in ((1, sum_x), (2, sum_far)):
        on_copies[j].wait_recv()
        g_sum[j - 1] = (g_own[j] + r_on_buf[j].astype(F32)).astype(BF16)
        copy.start()
    on_copies[0].wait_recv()
    mine = g_own[0] + r_on_buf[0].astype(F32)
    pl.when(inside)(lambda: wait_recv(across_grads))
    wait_recv([sum_x, sum_far])
    for i in range(5):
        mine = mine + r_buf[i].astype(F32)
    out[0] = mine[:, :t]
    out[1] = mine[:, t:]
    wait_send(first + meas_x + [fwd_x, fwd_far, sum_x, sum_far] + on_copies)
    wait_send(meas_own + sum(meas_fwd, []))
    pl.when(inside)(lambda: wait_send(across_copies + across_grads))


def per_device(n_r, n_c, tables, specimen, probe, measured, centers, counts, helpers):
    t = specimen.shape[1]
    modes, _, n, _ = probe.shape
    fwd, bwd = tables
    vmem = pl.BlockSpec(memory_space=pltpu.VMEM)
    smem = pl.BlockSpec(memory_space=pltpu.SMEM)
    hbm = pl.BlockSpec(memory_space=pl.ANY)
    dma = pltpu.SemaphoreType.DMA
    return pl.pallas_call(
        functools.partial(kernel, n_r, n_c),
        out_shape=jax.ShapeDtypeStruct(specimen.shape, F32),
        in_specs=[smem, vmem, smem, hbm, hbm, hbm, hbm, hbm],
        out_specs=vmem,
        scratch_shapes=[
            pltpu.VMEM(specimen.shape, F32),
            pltpu.VMEM((n, n), F32),
            pltpu.VMEM(probe.shape, F32),
            pltpu.VMEM((2 * n, 2 * n), BF16),
            pltpu.VMEM((2 * n, 2 * n), BF16),
            pltpu.VMEM((2, 8, 128), jnp.int32),
            pltpu.VMEM((9, t, 2 * t), BF16),
            pltpu.VMEM((n_c, CHUNKS, n // CHUNKS, n), BF16),
            pltpu.VMEM((2, modes * n, 2 * n), BF16),
            pltpu.VMEM((2, 2 * n, modes * n), BF16),
            pltpu.VMEM((2, 2 * n, modes * n), F32),
            pltpu.VMEM((3, 2 * n, 2 * t), BF16),
            pltpu.VMEM((3, t, 2 * t), F32),
            pltpu.VMEM((3, t, 2 * t), BF16),
            pltpu.VMEM((3, t, 2 * t), BF16),
            pltpu.VMEM((2, t, 2 * t), BF16),
            pltpu.VMEM((3, t, 2 * t), BF16),
            pltpu.VMEM((5, t, 2 * t), BF16),
            dma((5,)),
            dma((2,)),
            dma((9,)),
            dma((9,)),
            dma((CHUNKS + (CHUNKS + 1) * (n_c // 2 - 1),)),
            dma((CHUNKS + (CHUNKS + 1) * (n_c // 2 - 1),)),
            dma((8,)),
            dma((8,)),
        ],
        compiler_params=pltpu.CompilerParams(
            collective_id=0, has_side_effects=True, vmem_limit_bytes=56 * 1024 * 1024
        ),
    )(
        centers,
        counts,
        helpers,
        specimen,
        measured.reshape(n, n),
        probe,
        fwd,
        bwd,
    )


def solution(mesh):
    n_r, n_c = mesh.shape["row"], mesh.shape["col"]

    def program(specimen, probe, measured, centers, counts, helpers):
        base = dft_blocks(probe.shape[-1])
        tables = (jnp.asarray(base, BF16), jnp.asarray(base.T, BF16))
        return jax.shard_map(
            functools.partial(per_device, n_r, n_c, tables),
            mesh=mesh,
            in_specs=(
                P(None, "row", "col"),
                P(),
                P("row", "col", None, None, None),
                P("row", "col", None, None),
                P("row", "col"),
                P("row", "col", None),
            ),
            out_specs=P(None, "row", "col"),
            check_vma=False,
        )(specimen, probe, measured, centers, counts, helpers)

    return program
```

```python
import functools
import math

import jax
import jax.numpy as jnp
import numpy as np
from jax import lax
from jax.experimental import pallas as pl
from jax.experimental.pallas import tpu as pltpu
from jax.sharding import PartitionSpec as P

MESH = pl.DeviceIdType.MESH
F32 = jnp.float32
BF16 = jnp.bfloat16
CHUNKS = 4


def dft_blocks(extent):
    idx = np.arange(extent)
    angles = (idx[:, None] * idx[None, :] % extent) * (2.0 * math.pi / extent)
    scale = 1.0 / math.sqrt(extent)
    re, im = np.cos(angles) * scale, -np.sin(angles) * scale
    return np.block([[re, im], [-im, re]])


def dot(a, b):
    return jnp.dot(a, b, preferred_element_type=F32)


def kernel(
    n_r,
    n_c,
    centers,
    counts,
    helpers,
    spec_hbm,
    measured_hbm,
    probe_hbm,
    fwd_hbm,
    bwd_hbm,
    out,
    spec,
    measured,
    probe,
    fwd,
    bwd,
    meta,
    nb,
    meas,
    rows_buf,
    cols_buf,
    far,
    zbuf,
    g_own,
    g_on,
    g_off,
    g_sum,
    r_on_buf,
    r_buf,
    local_sem,
    meta_sem,
    halo_send,
    halo_recv,
    meas_send,
    meas_recv,
    grad_send,
    grad_recv,
):
    t = spec.shape[1]
    n = probe.shape[-1]
    modes = probe.shape[0]
    r, c = lax.axis_index("row"), lax.axis_index("col")
    odd_r, odd_c = lax.rem(r, 2), lax.rem(c, 2)
    r_on = r + 1 - 2 * odd_r
    r_off = lax.rem(r - 1 + 2 * odd_r + n_r, n_r)
    inside = (r > 0) & (r < n_r - 1)
    c_x = c + 1 - 2 * odd_c
    c_give = lax.rem(c - 2 + 4 * odd_c + n_c, n_c)
    c_take = lax.rem(c + 2 - 4 * odd_c + n_c, n_c)
    peers = [lax.rem(c + 2 * k, n_c) for k in range(1, n_c // 2)]

    barrier = pltpu.get_barrier_semaphore()
    near = [(r_on, c), (r, c_x)] + [(r, p) for p in peers]
    across = [(r_off, c), (r_off, c_x), (r_off, c_give), (r_off, c_take)]

    def greet(partners):
        for partner in partners:
            pl.semaphore_signal(barrier, inc=1, device_id=partner, device_id_type=MESH)

    greet(near)
    pl.when(inside)(lambda: greet(across))

    loads = [
        pltpu.make_async_copy(src, dst, local_sem.at[i])
        for i, (src, dst) in enumerate(
            [
                (spec_hbm, spec),
                (measured_hbm, measured),
                (probe_hbm, probe),
                (fwd_hbm, fwd),
                (bwd_hbm, bwd),
            ]
        )
    ]
    for load in loads:
        load.start()

    loads[0].wait()
    nb[0] = jnp.concatenate([spec[0], spec[1]], axis=1).astype(BF16)
    values = [centers[0, 0, i, j] for i in range(2) for j in range(2)]
    values += [helpers[0, 0, 0], helpers[0, 0, 1], counts[...]]
    which = lax.broadcasted_iota(jnp.int32, (8, 128), 0)
    block = jnp.zeros((8, 128), jnp.int32)
    for i, value in enumerate(values):
        block = jnp.where(which == i, value, block)
    meta[0] = block
    loads[1].wait()
    meas[c] = measured[...].astype(BF16).reshape(meas.shape[1:])

    @pl.when(jnp.logical_not(inside))
    def _():
        nb[6:9] = jnp.zeros((3, t, 2 * t), BF16)
        r_buf[0:3] = jnp.zeros((3, t, 2 * t), BF16)

    pl.semaphore_wait(barrier, len(near) + jnp.where(inside, len(across), 0))

    def remote(src, dst, send, recv, device):
        return pltpu.make_async_remote_copy(
            src_ref=src,
            dst_ref=dst,
            send_sem=send,
            recv_sem=recv,
            device_id=device,
            device_id_type=MESH,
        )

    def halo(src, dst, device):
        return remote(nb.at[src], nb.at[dst], halo_send.at[dst], halo_recv.at[dst], device)

    to_x = halo(0, 1, (r, c_x))
    to_off_x = halo(0, 7, (r_off, c_x))
    to_far = halo(0, 2, (r, c_give))
    to_off_far = halo(0, 8, (r_off, c_give))
    to_off = halo(0, 6, (r_off, c))
    to_on = halo(0, 3, (r_on, c))
    meta_copy = remote(meta.at[0], meta.at[1], meta_sem.at[0], meta_sem.at[1], (r, c_x))
    first = [meta_copy, to_x, to_far, to_on]
    across_copies = [to_off_x, to_off_far, to_off]

    def start(copies):
        for copy in copies:
            copy.start()

    def wait_recv(copies):
        for copy in copies:
            copy.wait_recv()

    def wait_send(copies):
        for copy in copies:
            copy.wait_send()

    start(first[:2])
    pl.when(inside)(lambda: start(across_copies))
    start(first[2:])

    chunks = meas.shape[1]
    sides = n_c // 2 - 1

    def meas_copy(src, sem, device):
        return remote(src, src, meas_send.at[sem], meas_recv.at[sem], device)

    meas_x = [meas_copy(meas.at[c, q], q, (r, c_x)) for q in range(chunks)]
    meas_own = [meas_copy(meas.at[c], chunks + k, (r, p)) for k, p in enumerate(peers)]
    meas_fwd = [
        [
            meas_copy(meas.at[c_x, q], chunks + sides * (q + 1) + k, (r, p))
            for k, p in enumerate(peers)
        ]
        for q in range(chunks)
    ]
    start(meas_x)
    start(meas_own)

    def pass_on(some):
        for q in some:
            meas_x[q].wait_recv()
            start(meas_fwd[q])

    to_x.wait_recv()
    fwd_x = halo(1, 4, (r_on, c))
    fwd_x.start()
    to_far.wait_recv()
    fwd_far = halo(2, 5, (r_on, c))
    fwd_far.start()

    meta_copy.wait_recv()
    info = meta[1]
    cr = [info[0:1, 0:1], info[2:3, 0:1]]
    cc = [info[1:2, 0:1], info[3:4, 0:1]]
    hc = [info[4:5, 0:1], info[5:6, 0:1]]
    live = [info[6:7, 0:1] > s for s in range(2)]

    nowhere = -4 * n
    row_on, row_off = 2 * t * (1 - odd_r), 2 * t * odd_r
    row_off = jnp.where((r == 0) | (r == n_r - 1), nowhere, row_off)
    col_own, col_far = 2 * t * odd_c, 2 * t * (1 - odd_c)
    col_far = jnp.where((c == 1) | (c == n_c - 2), nowhere, col_far)

    def place(idx, first_, second, third):
        role = idx // t
        base = jnp.where(role == 0, first_, jnp.where(role == 1, second, third))
        return base + idx - role * t

    def one_hot(shape, axis, roles, start):
        role_idx = lax.broadcasted_iota(jnp.int32, shape, axis)
        pix = lax.broadcasted_iota(jnp.int32, shape, 1 - axis)
        return jnp.where(place(role_idx, *roles) == pix + start, 1.0, 0.0).astype(BF16)

    row_roles = (t, row_on, row_off)
    col_roles = (col_own, t, col_far)
    row_at = [jnp.where(live[s], cr[s], 8 * n) for s in range(2)]

    pl.when(inside)(lambda: wait_recv(across_copies))
    wait_recv([to_on, fwd_x, fwd_far])
    for load in loads[2:]:
        load.wait()

    tiles = [jnp.concatenate([nb[j], nb[3 + j], nb[6 + j]], axis=0) for j in range(3)]

    for s in range(2):
        pick = one_hot((n, 3 * t), 1, row_roles, row_at[s])
        cut = [dot(pick, tiles[j]).astype(BF16) for j in range(3)]
        strip = jnp.concatenate(
            [
                jnp.concatenate([x[:, :t] for x in cut], axis=1),
                jnp.concatenate([x[:, t:] for x in cut], axis=1),
            ],
            axis=0,
        )
        patch = dot(strip, one_hot((3 * t, n), 0, col_roles, cc[s]))
        re, im = patch[:n], patch[n:]
        for k in range(modes):
            p_re, p_im = probe[k, 0], probe[k, 1]
            rows_buf[s, k * n : (k + 1) * n, :n] = (p_re * re - p_im * im).astype(BF16)
            rows_buf[s, k * n : (k + 1) * n, n:] = (p_re * im + p_im * re).astype(BF16)
        for k in range(modes):
            half = dot(rows_buf[s, k * n : (k + 1) * n], fwd[...]).astype(BF16)
            cols_buf[s, :n, k * n : (k + 1) * n] = half[:, :n]
            cols_buf[s, n:, k * n : (k + 1) * n] = half[:, n:]
        far[s] = dot(bwd[...], cols_buf[s])
        pass_on(range(s * chunks // 2, (s + 1) * chunks // 2))

    w = n // chunks
    wait_recv(meas_own)
    for q in range(chunks):
        wait_recv(meas_fwd[q])
        lo, block = q * w, modes * w
        for s in range(2):
            intensity = jnp.zeros((w, n), F32)
            for k in range(modes):
                f_re = far[s, lo : lo + w, k * n : (k + 1) * n]
                f_im = far[s, n + lo : n + lo + w, k * n : (k + 1) * n]
                intensity = intensity + (f_re * f_re + f_im * f_im)
            amp = jnp.zeros((w, n), F32)
            for h in range(n_c):
                amp = amp + jnp.where(hc[s] == h, meas[h, q].astype(F32), 0.0)
            factor = 1.0 - amp * lax.rsqrt(jnp.maximum(intensity, 0.25))
            for k in range(modes):
                at = q * block + k * w
                for part in range(2):
                    row = part * n + lo
                    f = far[s, row : row + w, k * n : (k + 1) * n]
                    rows_buf[s, at : at + w, part * n : (part + 1) * n] = (f * factor).astype(BF16)
            back = dot(rows_buf[s, q * block : (q + 1) * block], bwd[...]).astype(BF16)
            for k in range(modes):
                for part in range(2):
                    row = part * n + lo
                    cols_buf[s, row : row + w, k * n : (k + 1) * n] = back[
                        k * w : (k + 1) * w, part * n : (part + 1) * n
                    ]

    for s in range(2):
        far[s] = dot(fwd[...], cols_buf[s])
        g_re = jnp.zeros((n, n), F32)
        g_im = jnp.zeros((n, n), F32)
        for k in range(modes):
            p_re, p_im = probe[k, 0], probe[k, 1]
            x_re = far[s, :n, k * n : (k + 1) * n]
            x_im = far[s, n:, k * n : (k + 1) * n]
            g_re = g_re + (p_re * x_re + p_im * x_im)
            g_im = g_im + (p_re * x_im - p_im * x_re)
        grad = jnp.concatenate([g_re, g_im], axis=0).astype(BF16)
        wide = dot(grad, one_hot((n, 3 * t), 1, col_roles, cc[s])).astype(BF16)
        for j in range(3):
            zbuf[j, s * n : (s + 1) * n, :t] = wide[:n, j * t : (j + 1) * t]
            zbuf[j, s * n : (s + 1) * n, t:] = wide[n:, j * t : (j + 1) * t]

    spread = jnp.concatenate(
        [one_hot((3 * t, n), 0, row_roles, row_at[s]) for s in range(2)], axis=1
    )

    def grad_copy(src, dst, i, device):
        return remote(src, dst, grad_send.at[i], grad_recv.at[i], device)

    order = (1, 2, 0)
    on_copies = [grad_copy(g_on.at[j], r_on_buf.at[j], 5 + j, (r_on, c)) for j in range(3)]
    for j in order:
        g_on[j] = dot(spread[t : 2 * t], zbuf[j]).astype(BF16)
        on_copies[j].start()
    for j in order:
        g_off[j] = dot(spread[2 * t :], zbuf[j]).astype(BF16)
    off_x = grad_copy(g_off.at[1], r_buf.at[0], 0, (r_off, c_x))
    off_far = grad_copy(g_off.at[2], r_buf.at[1], 1, (r_off, c_take))
    off_own = grad_copy(g_off.at[0], r_buf.at[2], 2, (r_off, c))
    across_grads = [off_x, off_far, off_own]
    pl.when(inside)(lambda: start(across_grads))
    for j in order:
        g_own[j] = dot(spread[:t], zbuf[j])
    sum_x = grad_copy(g_sum.at[0], r_buf.at[3], 3, (r, c_x))
    sum_far = grad_copy(g_sum.at[1], r_buf.at[4], 4, (r, c_take))
    for j, copy in ((1, sum_x), (2, sum_far)):
        on_copies[j].wait_recv()
        g_sum[j - 1] = (g_own[j] + r_on_buf[j].astype(F32)).astype(BF16)
        copy.start()
    on_copies[0].wait_recv()
    mine = g_own[0] + r_on_buf[0].astype(F32)
    pl.when(inside)(lambda: wait_recv(across_grads))
    wait_recv([sum_x, sum_far])
    for i in range(5):
        mine = mine + r_buf[i].astype(F32)
    out[0] = mine[:, :t]
    out[1] = mine[:, t:]
    wait_send(first + meas_x + [fwd_x, fwd_far, sum_x, sum_far] + on_copies)
    wait_send(meas_own + sum(meas_fwd, []))
    pl.when(inside)(lambda: wait_send(across_copies + across_grads))


def per_device(n_r, n_c, tables, specimen, probe, measured, centers, counts, helpers):
    t = specimen.shape[1]
    modes, _, n, _ = probe.shape
    fwd, bwd = tables
    vmem = pl.BlockSpec(memory_space=pltpu.VMEM)
    smem = pl.BlockSpec(memory_space=pltpu.SMEM)
    hbm = pl.BlockSpec(memory_space=pl.ANY)
    dma = pltpu.SemaphoreType.DMA
    return pl.pallas_call(
        functools.partial(kernel, n_r, n_c),
        out_shape=pltpu.VMEM(specimen.shape, F32),
        in_specs=[smem, vmem, smem, hbm, hbm, hbm, hbm, hbm],
        out_specs=vmem,
        scratch_shapes=[
            pltpu.VMEM(specimen.shape, F32),
            pltpu.VMEM((n, n), F32),
            pltpu.VMEM(probe.shape, F32),
            pltpu.VMEM((2 * n, 2 * n), BF16),
            pltpu.VMEM((2 * n, 2 * n), BF16),
            pltpu.VMEM((2, 8, 128), jnp.int32),
            pltpu.VMEM((9, t, 2 * t), BF16),
            pltpu.VMEM((n_c, CHUNKS, n // CHUNKS, n), BF16),
            pltpu.VMEM((2, modes * n, 2 * n), BF16),
            pltpu.VMEM((2, 2 * n, modes * n), BF16),
            pltpu.VMEM((2, 2 * n, modes * n), F32),
            pltpu.VMEM((3, 2 * n, 2 * t), BF16),
            pltpu.VMEM((3, t, 2 * t), F32),
            pltpu.VMEM((3, t, 2 * t), BF16),
            pltpu.VMEM((3, t, 2 * t), BF16),
            pltpu.VMEM((2, t, 2 * t), BF16),
            pltpu.VMEM((3, t, 2 * t), BF16),
            pltpu.VMEM((5, t, 2 * t), BF16),
            dma((5,)),
            dma((2,)),
            dma((9,)),
            dma((9,)),
            dma((CHUNKS + (CHUNKS + 1) * (n_c // 2 - 1),)),
            dma((CHUNKS + (CHUNKS + 1) * (n_c // 2 - 1),)),
            dma((8,)),
            dma((8,)),
        ],
        compiler_params=pltpu.CompilerParams(
            collective_id=0, has_side_effects=True, vmem_limit_bytes=56 * 1024 * 1024
        ),
    )(
        centers,
        counts,
        helpers,
        specimen,
        measured.reshape(n, n),
        probe,
        fwd,
        bwd,
    )


def solution(mesh):
    n_r, n_c = mesh.shape["row"], mesh.shape["col"]

    def program(specimen, probe, measured, centers, counts, helpers):
        base = dft_blocks(probe.shape[-1])
        tables = (jnp.asarray(base, BF16), jnp.asarray(base.T, BF16))
        return jax.shard_map(
            functools.partial(per_device, n_r, n_c, tables),
            mesh=mesh,
            in_specs=(
                P(None, "row", "col"),
                P(),
                P("row", "col", None, None, None),
                P("row", "col", None, None),
                P("row", "col"),
                P("row", "col", None),
            ),
            out_specs=P(None, "row", "col"),
            check_vma=False,
        )(specimen, probe, measured, centers, counts, helpers)

    return program
```

```python
import functools
import math

import jax
import jax.numpy as jnp
import numpy as np
from jax import lax
from jax.experimental import pallas as pl
from jax.experimental.pallas import tpu as pltpu
from jax.sharding import PartitionSpec as P

MESH = pl.DeviceIdType.MESH
F32 = jnp.float32
BF16 = jnp.bfloat16
CHUNKS = 4


def dft_blocks(extent):
    idx = np.arange(extent)
    angles = (idx[:, None] * idx[None, :] % extent) * (2.0 * math.pi / extent)
    scale = 1.0 / math.sqrt(extent)
    re, im = np.cos(angles) * scale, -np.sin(angles) * scale
    return np.block([[re, im], [-im, re]])


def dot(a, b):
    return jnp.dot(a, b, preferred_element_type=F32)


def kernel(
    n_r,
    n_c,
    centers_hbm,
    counts_hbm,
    helpers_hbm,
    spec_hbm,
    measured_hbm,
    probe_hbm,
    fwd_hbm,
    bwd_hbm,
    out,
    centers,
    counts,
    helpers,
    spec,
    measured,
    probe,
    fwd,
    bwd,
    meta,
    nb,
    meas,
    rows_buf,
    cols_buf,
    far,
    chi,
    zbuf,
    g_own,
    g_on,
    g_off,
    g_sum,
    r_on_buf,
    r_buf,
    local_sem,
    meta_sem,
    halo_send,
    halo_recv,
    meas_send,
    meas_recv,
    grad_send,
    grad_recv,
):
    t = spec.shape[1]
    n = probe.shape[-1]
    modes = probe.shape[0]
    r, c = lax.axis_index("row"), lax.axis_index("col")
    odd_r, odd_c = lax.rem(r, 2), lax.rem(c, 2)
    r_on = r + 1 - 2 * odd_r
    r_off = lax.rem(r - 1 + 2 * odd_r + n_r, n_r)
    inside = (r > 0) & (r < n_r - 1)
    c_x = c + 1 - 2 * odd_c
    c_give = lax.rem(c - 2 + 4 * odd_c + n_c, n_c)
    c_take = lax.rem(c + 2 - 4 * odd_c + n_c, n_c)
    peers = [lax.rem(c + 2 * k, n_c) for k in range(1, n_c // 2)]

    barrier = pltpu.get_barrier_semaphore()
    near = [(r_on, c), (r, c_x)] + [(r, p) for p in peers]
    across = [(r_off, c), (r_off, c_x), (r_off, c_give), (r_off, c_take)]

    def greet(partners):
        for partner in partners:
            pl.semaphore_signal(barrier, inc=1, device_id=partner, device_id_type=MESH)

    greet(near)
    pl.when(inside)(lambda: greet(across))

    loads = [
        pltpu.make_async_copy(src, dst, local_sem.at[i])
        for i, (src, dst) in enumerate(
            [
                (spec_hbm, spec),
                (centers_hbm, centers),
                (counts_hbm, counts),
                (helpers_hbm, helpers),
                (measured_hbm, measured),
                (probe_hbm, probe),
                (fwd_hbm, fwd),
                (bwd_hbm, bwd),
            ]
        )
    ]
    for load in loads:
        load.start()

    loads[0].wait()
    nb[0] = jnp.concatenate([spec[0], spec[1]], axis=1).astype(BF16)
    for load in loads[1:4]:
        load.wait()
    at, to = centers[0, 0], helpers[0]
    values = [at[i : i + 1, j : j + 1] for i in range(2) for j in range(2)]
    values += [to[:, 0:1], to[:, 1:2], counts[...]]
    which = lax.broadcasted_iota(jnp.int32, (8, 128), 0)
    block = jnp.zeros((8, 128), jnp.int32)
    for i, value in enumerate(values):
        block = jnp.where(which == i, value, block)
    meta[0] = block
    loads[4].wait()
    meas[c] = measured[...].astype(BF16).reshape(meas.shape[1:])

    @pl.when(jnp.logical_not(inside))
    def _():
        nb[6:9] = jnp.zeros((3, t, 2 * t), BF16)
        r_buf[0:3] = jnp.zeros((3, t, 2 * t), BF16)

    pl.semaphore_wait(barrier, len(near) + jnp.where(inside, len(across), 0))

    def remote(src, dst, send, recv, device):
        return pltpu.make_async_remote_copy(
            src_ref=src,
            dst_ref=dst,
            send_sem=send,
            recv_sem=recv,
            device_id=device,
            device_id_type=MESH,
        )

    def halo(src, dst, device):
        return remote(nb.at[src], nb.at[dst], halo_send.at[dst], halo_recv.at[dst], device)

    to_x = halo(0, 1, (r, c_x))
    to_off_x = halo(0, 7, (r_off, c_x))
    to_far = halo(0, 2, (r, c_give))
    to_off_far = halo(0, 8, (r_off, c_give))
    to_off = halo(0, 6, (r_off, c))
    to_on = halo(0, 3, (r_on, c))
    meta_copy = remote(meta.at[0], meta.at[1], meta_sem.at[0], meta_sem.at[1], (r, c_x))
    first = [meta_copy, to_x, to_far, to_on]
    across_copies = [to_off_x, to_off_far, to_off]

    def start(copies):
        for copy in copies:
            copy.start()

    def wait_recv(copies):
        for copy in copies:
            copy.wait_recv()

    def wait_send(copies):
        for copy in copies:
            copy.wait_send()

    start(first[:2])
    pl.when(inside)(lambda: start(across_copies))
    start(first[2:])

    chunks = meas.shape[1]
    sides = n_c // 2 - 1

    def meas_copy(src, sem, device):
        return remote(src, src, meas_send.at[sem], meas_recv.at[sem], device)

    meas_x = [meas_copy(meas.at[c, q], q, (r, c_x)) for q in range(chunks)]
    meas_own = [meas_copy(meas.at[c], chunks + k, (r, p)) for k, p in enumerate(peers)]
    meas_fwd = [
        [
            meas_copy(meas.at[c_x, q], chunks + sides * (q + 1) + k, (r, p))
            for k, p in enumerate(peers)
        ]
        for q in range(chunks)
    ]
    start(meas_x)
    start(meas_own)

    def pass_on(some):
        for q in some:
            meas_x[q].wait_recv()
            start(meas_fwd[q])

    to_x.wait_recv()
    fwd_x = halo(1, 4, (r_on, c))
    fwd_x.start()
    to_far.wait_recv()
    fwd_far = halo(2, 5, (r_on, c))
    fwd_far.start()

    meta_copy.wait_recv()
    info = meta[1]
    cr = [info[0:1, 0:1], info[2:3, 0:1]]
    cc = [info[1:2, 0:1], info[3:4, 0:1]]
    hc = [info[4:5, 0:1], info[5:6, 0:1]]
    live = [info[6:7, 0:1] > s for s in range(2)]

    nowhere = -4 * n
    row_on, row_off = 2 * t * (1 - odd_r), 2 * t * odd_r
    row_off = jnp.where((r == 0) | (r == n_r - 1), nowhere, row_off)
    col_own, col_far = 2 * t * odd_c, 2 * t * (1 - odd_c)
    col_far = jnp.where((c == 1) | (c == n_c - 2), nowhere, col_far)

    def place(idx, first_, second, third):
        role = idx // t
        base = jnp.where(role == 0, first_, jnp.where(role == 1, second, third))
        return base + idx - role * t

    def one_hot(shape, axis, roles, start):
        role_idx = lax.broadcasted_iota(jnp.int32, shape, axis)
        pix = lax.broadcasted_iota(jnp.int32, shape, 1 - axis)
        return jnp.where(place(role_idx, *roles) == pix + start, 1.0, 0.0).astype(BF16)

    row_roles = (t, row_on, row_off)
    col_roles = (col_own, t, col_far)
    row_at = [jnp.where(live[s], cr[s], 8 * n) for s in range(2)]

    pl.when(inside)(lambda: wait_recv(across_copies))
    wait_recv([to_on, fwd_x, fwd_far])
    for load in loads[5:]:
        load.wait()

    tiles = [jnp.concatenate([nb[j], nb[3 + j], nb[6 + j]], axis=0) for j in range(3)]

    for s in range(2):
        pick = one_hot((n, 3 * t), 1, row_roles, row_at[s])
        cut = [dot(pick, tiles[j]).astype(BF16) for j in range(3)]
        strip = jnp.concatenate(
            [
                jnp.concatenate([x[:, :t] for x in cut], axis=1),
                jnp.concatenate([x[:, t:] for x in cut], axis=1),
            ],
            axis=0,
        )
        patch = dot(strip, one_hot((3 * t, n), 0, col_roles, cc[s]))
        re, im = patch[:n], patch[n:]
        for k in range(modes):
            p_re, p_im = probe[k, 0], probe[k, 1]
            rows_buf[s, k * n : (k + 1) * n, :n] = (p_re * re - p_im * im).astype(BF16)
            rows_buf[s, k * n : (k + 1) * n, n:] = (p_re * im + p_im * re).astype(BF16)
        for k in range(modes):
            half = dot(rows_buf[s, k * n : (k + 1) * n], fwd[...]).astype(BF16)
            cols_buf[s, :n, k * n : (k + 1) * n] = half[:, :n]
            cols_buf[s, n:, k * n : (k + 1) * n] = half[:, n:]
        far[s] = dot(bwd[...], cols_buf[s])
        pass_on(range(s * chunks // 2, (s + 1) * chunks // 2))

    w = n // chunks
    halves = [
        jnp.concatenate([fwd[:, i * t : (i + 1) * t], fwd[:, n + i * t : n + (i + 1) * t]], axis=1)
        for i in range(2)
    ]
    wait_recv(meas_own)
    for q in range(chunks):
        wait_recv(meas_fwd[q])
        lo, block = q * w, modes * w
        for s in range(2):
            intensity = jnp.zeros((w, n), F32)
            for k in range(modes):
                f_re = far[s, lo : lo + w, k * n : (k + 1) * n]
                f_im = far[s, n + lo : n + lo + w, k * n : (k + 1) * n]
                intensity = intensity + (f_re * f_re + f_im * f_im)
            amp = jnp.zeros((w, n), F32)
            for h in range(n_c):
                amp = amp + jnp.where(hc[s] == h, meas[h, q].astype(F32), 0.0)
            factor = 1.0 - amp * lax.rsqrt(jnp.maximum(intensity, 0.25))
            for k in range(modes):
                at = q * block + k * w
                for part in range(2):
                    row = part * n + lo
                    f = far[s, row : row + w, k * n : (k + 1) * n]
                    rows_buf[s, at : at + w, part * n : (part + 1) * n] = (f * factor).astype(BF16)
            back = dot(rows_buf[s, q * block : (q + 1) * block], bwd[...]).astype(BF16)
            for k in range(modes):
                for part in range(2):
                    row = lo // t * n + part * t + lo % t
                    cols_buf[s, row : row + w, k * n : (k + 1) * n] = back[
                        k * w : (k + 1) * w, part * n : (part + 1) * n
                    ]

        if q == chunks // 2 - 1:
            for s in range(2):
                chi[s] = dot(halves[0], cols_buf[s, :n])

    for s in range(2):
        chi[s] = chi[s] + dot(halves[1], cols_buf[s, n:])
        g_re = jnp.zeros((n, n), F32)
        g_im = jnp.zeros((n, n), F32)
        for k in range(modes):
            p_re, p_im = probe[k, 0], probe[k, 1]
            x_re = chi[s, :n, k * n : (k + 1) * n]
            x_im = chi[s, n:, k * n : (k + 1) * n]
            g_re = g_re + (p_re * x_re + p_im * x_im)
            g_im = g_im + (p_re * x_im - p_im * x_re)
        grad = jnp.concatenate([g_re, g_im], axis=0).astype(BF16)
        wide = dot(grad, one_hot((n, 3 * t), 1, col_roles, cc[s])).astype(BF16)
        for j in range(3):
            zbuf[j, s * n : (s + 1) * n, :t] = wide[:n, j * t : (j + 1) * t]
            zbuf[j, s * n : (s + 1) * n, t:] = wide[n:, j * t : (j + 1) * t]

    spread = jnp.concatenate(
        [one_hot((3 * t, n), 0, row_roles, row_at[s]) for s in range(2)], axis=1
    )

    def grad_copy(src, dst, i, device):
        return remote(src, dst, grad_send.at[i], grad_recv.at[i], device)

    order = (1, 2, 0)
    on_copies = [grad_copy(g_on.at[j], r_on_buf.at[j], 5 + j, (r_on, c)) for j in range(3)]
    for j in order:
        g_on[j] = dot(spread[t : 2 * t], zbuf[j]).astype(BF16)
        on_copies[j].start()
    for j in order:
        g_off[j] = dot(spread[2 * t :], zbuf[j]).astype(BF16)
    off_x = grad_copy(g_off.at[1], r_buf.at[0], 0, (r_off, c_x))
    off_far = grad_copy(g_off.at[2], r_buf.at[1], 1, (r_off, c_take))
    off_own = grad_copy(g_off.at[0], r_buf.at[2], 2, (r_off, c))
    across_grads = [off_x, off_far, off_own]
    pl.when(inside)(lambda: start(across_grads[:1]))
    for j in order:
        g_own[j] = dot(spread[:t], zbuf[j])
    sum_x = grad_copy(g_sum.at[0], r_buf.at[3], 3, (r, c_x))
    sum_far = grad_copy(g_sum.at[1], r_buf.at[4], 4, (r, c_take))
    for j, copy in ((1, sum_x), (2, sum_far)):
        on_copies[j].wait_recv()
        g_sum[j - 1] = (g_own[j] + r_on_buf[j].astype(F32)).astype(BF16)
        copy.start()
    pl.when(inside)(lambda: start(across_grads[1:]))
    on_copies[0].wait_recv()
    mine = g_own[0] + r_on_buf[0].astype(F32)
    pl.when(inside)(lambda: wait_recv(across_grads))
    wait_recv([sum_x, sum_far])
    for i in range(5):
        mine = mine + r_buf[i].astype(F32)
    out[0] = mine[:, :t]
    out[1] = mine[:, t:]
    wait_send(first + meas_x + [fwd_x, fwd_far, sum_x, sum_far] + on_copies)
    wait_send(meas_own + sum(meas_fwd, []))
    pl.when(inside)(lambda: wait_send(across_copies + across_grads))


def per_device(n_r, n_c, tables, specimen, probe, measured, centers, counts, helpers):
    t = specimen.shape[1]
    modes, _, n, _ = probe.shape
    fwd, bwd = tables
    vmem = pl.BlockSpec(memory_space=pltpu.VMEM)
    hbm = pl.BlockSpec(memory_space=pl.ANY)
    dma = pltpu.SemaphoreType.DMA
    return pl.pallas_call(
        functools.partial(kernel, n_r, n_c),
        out_shape=pltpu.VMEM(specimen.shape, F32),
        in_specs=[hbm] * 8,
        out_specs=vmem,
        scratch_shapes=[
            pltpu.VMEM(centers.shape, jnp.int32),
            pltpu.VMEM(counts.shape, jnp.int32),
            pltpu.VMEM(helpers.shape, jnp.int32),
            pltpu.VMEM(specimen.shape, F32),
            pltpu.VMEM((n, n), F32),
            pltpu.VMEM(probe.shape, F32),
            pltpu.VMEM((2 * n, 2 * n), BF16),
            pltpu.VMEM((2 * n, 2 * n), BF16),
            pltpu.VMEM((2, 8, 128), jnp.int32),
            pltpu.VMEM((9, t, 2 * t), BF16),
            pltpu.VMEM((n_c, CHUNKS, n // CHUNKS, n), BF16),
            pltpu.VMEM((2, modes * n, 2 * n), BF16),
            pltpu.VMEM((2, 2 * n, modes * n), BF16),
            pltpu.VMEM((2, 2 * n, modes * n), F32),
            pltpu.VMEM((2, 2 * n, modes * n), F32),
            pltpu.VMEM((3, 2 * n, 2 * t), BF16),
            pltpu.VMEM((3, t, 2 * t), F32),
            pltpu.VMEM((3, t, 2 * t), BF16),
            pltpu.VMEM((3, t, 2 * t), BF16),
            pltpu.VMEM((2, t, 2 * t), BF16),
            pltpu.VMEM((3, t, 2 * t), BF16),
            pltpu.VMEM((5, t, 2 * t), BF16),
            dma((8,)),
            dma((2,)),
            dma((9,)),
            dma((9,)),
            dma((CHUNKS + (CHUNKS + 1) * (n_c // 2 - 1),)),
            dma((CHUNKS + (CHUNKS + 1) * (n_c // 2 - 1),)),
            dma((8,)),
            dma((8,)),
        ],
        compiler_params=pltpu.CompilerParams(
            collective_id=0, has_side_effects=True, vmem_limit_bytes=56 * 1024 * 1024
        ),
    )(
        centers,
        counts,
        helpers,
        specimen,
        measured.reshape(n, n),
        probe,
        fwd,
        bwd,
    )


def solution(mesh):
    n_r, n_c = mesh.shape["row"], mesh.shape["col"]

    def program(specimen, probe, measured, centers, counts, helpers):
        base = dft_blocks(probe.shape[-1])
        tables = (jnp.asarray(base, BF16), jnp.asarray(base.T, BF16))
        return jax.shard_map(
            functools.partial(per_device, n_r, n_c, tables),
            mesh=mesh,
            in_specs=(
                P(None, "row", "col"),
                P(),
                P("row", "col", None, None, None),
                P("row", "col", None, None),
                P("row", "col"),
                P("row", "col", None),
            ),
            out_specs=P(None, "row", "col"),
            check_vma=False,
        )(specimen, probe, measured, centers, counts, helpers)

    return program
```

```python
import functools
import math

import jax
import jax.numpy as jnp
import numpy as np
from jax import lax
from jax.experimental import pallas as pl
from jax.experimental.pallas import tpu as pltpu
from jax.sharding import PartitionSpec as P

MESH = pl.DeviceIdType.MESH
F32 = jnp.float32
BF16 = jnp.bfloat16
CHUNKS = 4


def dft_blocks(extent):
    idx = np.arange(extent)
    angles = (idx[:, None] * idx[None, :] % extent) * (2.0 * math.pi / extent)
    scale = 1.0 / math.sqrt(extent)
    re, im = np.cos(angles) * scale, -np.sin(angles) * scale
    return np.block([[re, im], [-im, re]])


def dot(a, b):
    return jnp.dot(a, b, preferred_element_type=F32)


def kernel(
    n_r,
    n_c,
    centers_hbm,
    counts_hbm,
    helpers_hbm,
    spec_hbm,
    measured_hbm,
    probe_hbm,
    fwd_hbm,
    bwd_hbm,
    out,
    centers,
    counts,
    helpers,
    spec,
    measured,
    probe,
    fwd,
    bwd,
    meta,
    nb,
    meas,
    rows_buf,
    cols_buf,
    far,
    chi,
    zbuf,
    g_own,
    g_on,
    g_off,
    g_sum,
    r_on_buf,
    r_buf,
    local_sem,
    meta_sem,
    halo_send,
    halo_recv,
    meas_send,
    meas_recv,
    grad_send,
    grad_recv,
):
    t = spec.shape[1]
    n = probe.shape[-1]
    modes = probe.shape[0]
    r, c = lax.axis_index("row"), lax.axis_index("col")
    odd_r, odd_c = lax.rem(r, 2), lax.rem(c, 2)
    r_on = r + 1 - 2 * odd_r
    r_off = lax.rem(r - 1 + 2 * odd_r + n_r, n_r)
    inside = (r > 0) & (r < n_r - 1)
    gives = (c > 0) & (c < n_c - 1)
    takes = (c != 1) & (c != n_c - 2)
    c_x = c + 1 - 2 * odd_c
    c_give = lax.rem(c - 2 + 4 * odd_c + n_c, n_c)
    c_take = lax.rem(c + 2 - 4 * odd_c + n_c, n_c)
    peers = [lax.rem(c + 2 * k, n_c) for k in range(1, n_c // 2)]

    barrier = pltpu.get_barrier_semaphore()
    near = [(r_on, c), (r, c_x)] + [(r, p) for p in peers]
    across = [(r_off, c), (r_off, c_x)]

    def greet(partners):
        for partner in partners:
            pl.semaphore_signal(barrier, inc=1, device_id=partner, device_id_type=MESH)

    greet(near)
    pl.when(inside)(lambda: greet(across))
    pl.when(inside & gives)(lambda: greet([(r_off, c_give)]))
    pl.when(inside & takes)(lambda: greet([(r_off, c_take)]))

    loads = [
        pltpu.make_async_copy(src, dst, local_sem.at[i])
        for i, (src, dst) in enumerate(
            [
                (spec_hbm, spec),
                (centers_hbm, centers),
                (counts_hbm, counts),
                (helpers_hbm, helpers),
                (measured_hbm, measured),
                (probe_hbm, probe),
                (fwd_hbm, fwd),
                (bwd_hbm, bwd),
            ]
        )
    ]
    for load in loads:
        load.start()

    loads[0].wait()
    nb[0] = jnp.concatenate([spec[0], spec[1]], axis=1).astype(BF16)
    for load in loads[1:4]:
        load.wait()
    at, to = centers[0, 0], helpers[0]
    values = [at[i : i + 1, j : j + 1] for i in range(2) for j in range(2)]
    values += [to[:, 0:1], to[:, 1:2], counts[...]]
    which = lax.broadcasted_iota(jnp.int32, (8, 128), 0)
    block = jnp.zeros((8, 128), jnp.int32)
    for i, value in enumerate(values):
        block = jnp.where(which == i, value, block)
    meta[0] = block
    loads[4].wait()
    meas[c] = measured[...].astype(BF16).reshape(meas.shape[1:])

    @pl.when(jnp.logical_not(inside))
    def _():
        nb[6:9] = jnp.zeros((3, t, 2 * t), BF16)
        r_buf[0:3] = jnp.zeros((3, t, 2 * t), BF16)

    @pl.when(jnp.logical_not(takes))
    def _():
        for i in (2, 5, 8):
            nb[i] = jnp.zeros((t, 2 * t), BF16)

    @pl.when(jnp.logical_not(gives))
    def _():
        for i in (1, 4):
            r_buf[i] = jnp.zeros((t, 2 * t), BF16)

    over = len(across) + jnp.where(gives, 1, 0) + jnp.where(takes, 1, 0)
    pl.semaphore_wait(barrier, len(near) + jnp.where(inside, over, 0))

    def remote(src, dst, send, recv, device):
        return pltpu.make_async_remote_copy(
            src_ref=src,
            dst_ref=dst,
            send_sem=send,
            recv_sem=recv,
            device_id=device,
            device_id_type=MESH,
        )

    def halo(src, dst, device):
        return remote(nb.at[src], nb.at[dst], halo_send.at[dst], halo_recv.at[dst], device)

    to_x = halo(0, 1, (r, c_x))
    to_off_x = halo(0, 7, (r_off, c_x))
    to_far = halo(0, 2, (r, c_give))
    to_off_far = halo(0, 8, (r_off, c_give))
    to_off = halo(0, 6, (r_off, c))
    to_on = halo(0, 3, (r_on, c))
    meta_copy = remote(meta.at[0], meta.at[1], meta_sem.at[0], meta_sem.at[1], (r, c_x))
    first = [meta_copy, to_x, to_on]
    across_copies = [to_off_x, to_off]

    def start(copies):
        for copy in copies:
            copy.start()

    def wait_recv(copies):
        for copy in copies:
            copy.wait_recv()

    def wait_send(copies):
        for copy in copies:
            copy.wait_send()

    start(first[:2])
    pl.when(inside)(lambda: start(across_copies))
    pl.when(inside & gives)(lambda: start([to_off_far]))
    pl.when(gives)(lambda: start([to_far]))
    start(first[2:])

    chunks = meas.shape[1]
    sides = n_c // 2 - 1

    def meas_copy(src, sem, device):
        return remote(src, src, meas_send.at[sem], meas_recv.at[sem], device)

    meas_x = [meas_copy(meas.at[c, q], q, (r, c_x)) for q in range(chunks)]
    meas_own = [meas_copy(meas.at[c], chunks + k, (r, p)) for k, p in enumerate(peers)]
    meas_fwd = [
        [
            meas_copy(meas.at[c_x, q], chunks + sides * (q + 1) + k, (r, p))
            for k, p in enumerate(peers)
        ]
        for q in range(chunks)
    ]
    start(meas_x)
    start(meas_own)

    def pass_on(some):
        for q in some:
            meas_x[q].wait_recv()
            start(meas_fwd[q])

    to_x.wait_recv()
    fwd_x = halo(1, 4, (r_on, c))
    fwd_x.start()
    fwd_far = halo(2, 5, (r_on, c))

    @pl.when(takes)
    def _():
        to_far.wait_recv()
        fwd_far.start()


    meta_copy.wait_recv()
    info = meta[1]
    cr = [info[0:1, 0:1], info[2:3, 0:1]]
    cc = [info[1:2, 0:1], info[3:4, 0:1]]
    hc = [info[4:5, 0:1], info[5:6, 0:1]]
    live = [info[6:7, 0:1] > s for s in range(2)]

    nowhere = -4 * n
    row_on, row_off = 2 * t * (1 - odd_r), 2 * t * odd_r
    row_off = jnp.where((r == 0) | (r == n_r - 1), nowhere, row_off)
    col_own, col_far = 2 * t * odd_c, 2 * t * (1 - odd_c)
    col_far = jnp.where((c == 1) | (c == n_c - 2), nowhere, col_far)

    def place(idx, first_, second, third):
        role = idx // t
        base = jnp.where(role == 0, first_, jnp.where(role == 1, second, third))
        return base + idx - role * t

    def one_hot(shape, axis, roles, start):
        role_idx = lax.broadcasted_iota(jnp.int32, shape, axis)
        pix = lax.broadcasted_iota(jnp.int32, shape, 1 - axis)
        return jnp.where(place(role_idx, *roles) == pix + start, 1.0, 0.0).astype(BF16)

    row_roles = (t, row_on, row_off)
    col_roles = (col_own, t, col_far)
    row_at = [jnp.where(live[s], cr[s], 8 * n) for s in range(2)]

    pl.when(inside)(lambda: wait_recv(across_copies))
    pl.when(inside & takes)(lambda: wait_recv([to_off_far]))
    pl.when(takes)(lambda: wait_recv([fwd_far]))
    wait_recv([to_on, fwd_x])
    for load in loads[5:]:
        load.wait()

    tiles = [jnp.concatenate([nb[j], nb[3 + j], nb[6 + j]], axis=0) for j in range(3)]

    for s in range(2):
        pick = one_hot((n, 3 * t), 1, row_roles, row_at[s])
        cut = [dot(pick, tiles[j]).astype(BF16) for j in range(3)]
        strip = jnp.concatenate(
            [
                jnp.concatenate([x[:, :t] for x in cut], axis=1),
                jnp.concatenate([x[:, t:] for x in cut], axis=1),
            ],
            axis=0,
        )
        patch = dot(strip, one_hot((3 * t, n), 0, col_roles, cc[s]))
        re, im = patch[:n], patch[n:]
        for k in range(modes):
            p_re, p_im = probe[k, 0], probe[k, 1]
            rows_buf[s, k * n : (k + 1) * n, :n] = (p_re * re - p_im * im).astype(BF16)
            rows_buf[s, k * n : (k + 1) * n, n:] = (p_re * im + p_im * re).astype(BF16)
        for k in range(modes):
            half = dot(rows_buf[s, k * n : (k + 1) * n], fwd[...]).astype(BF16)
            cols_buf[s, :n, k * n : (k + 1) * n] = half[:, :n]
            cols_buf[s, n:, k * n : (k + 1) * n] = half[:, n:]
        far[s] = dot(bwd[...], cols_buf[s])
        pass_on(range(s * chunks // 2, (s + 1) * chunks // 2))

    w = n // chunks
    halves = [
        jnp.concatenate([fwd[:, i * t : (i + 1) * t], fwd[:, n + i * t : n + (i + 1) * t]], axis=1)
        for i in range(2)
    ]
    wait_recv(meas_own)
    for q in range(chunks):
        wait_recv(meas_fwd[q])
        lo, block = q * w, modes * w
        for s in range(2):
            intensity = jnp.zeros((w, n), F32)
            for k in range(modes):
                f_re = far[s, lo : lo + w, k * n : (k + 1) * n]
                f_im = far[s, n + lo : n + lo + w, k * n : (k + 1) * n]
                intensity = intensity + (f_re * f_re + f_im * f_im)
            amp = jnp.zeros((w, n), F32)
            for h in range(n_c):
                amp = amp + jnp.where(hc[s] == h, meas[h, q].astype(F32), 0.0)
            factor = 1.0 - amp * lax.rsqrt(jnp.maximum(intensity, 0.25))
            for k in range(modes):
                at = q * block + k * w
                for part in range(2):
                    row = part * n + lo
                    f = far[s, row : row + w, k * n : (k + 1) * n]
                    rows_buf[s, at : at + w, part * n : (part + 1) * n] = (f * factor).astype(BF16)
            back = dot(rows_buf[s, q * block : (q + 1) * block], bwd[...]).astype(BF16)
            for k in range(modes):
                for part in range(2):
                    row = lo // t * n + part * t + lo % t
                    cols_buf[s, row : row + w, k * n : (k + 1) * n] = back[
                        k * w : (k + 1) * w, part * n : (part + 1) * n
                    ]

        if q == chunks // 2 - 1:
            for s in range(2):
                chi[s] = dot(halves[0], cols_buf[s, :n])

    for s in range(2):
        chi[s] = chi[s] + dot(halves[1], cols_buf[s, n:])
        g_re = jnp.zeros((n, n), F32)
        g_im = jnp.zeros((n, n), F32)
        for k in range(modes):
            p_re, p_im = probe[k, 0], probe[k, 1]
            x_re = chi[s, :n, k * n : (k + 1) * n]
            x_im = chi[s, n:, k * n : (k + 1) * n]
            g_re = g_re + (p_re * x_re + p_im * x_im)
            g_im = g_im + (p_re * x_im - p_im * x_re)
        grad = jnp.concatenate([g_re, g_im], axis=0).astype(BF16)
        wide = dot(grad, one_hot((n, 3 * t), 1, col_roles, cc[s])).astype(BF16)
        for j in range(3):
            zbuf[j, s * n : (s + 1) * n, :t] = wide[:n, j * t : (j + 1) * t]
            zbuf[j, s * n : (s + 1) * n, t:] = wide[n:, j * t : (j + 1) * t]

    spread = jnp.concatenate(
        [one_hot((3 * t, n), 0, row_roles, row_at[s]) for s in range(2)], axis=1
    )

    def grad_copy(src, dst, i, device):
        return remote(src, dst, grad_send.at[i], grad_recv.at[i], device)

    order = (1, 2, 0)
    on_copies = [grad_copy(g_on.at[j], r_on_buf.at[j], 5 + j, (r_on, c)) for j in range(3)]
    for j in order:
        g_on[j] = dot(spread[t : 2 * t], zbuf[j]).astype(BF16)
        on_copies[j].start()
    for j in order:
        g_off[j] = dot(spread[2 * t :], zbuf[j]).astype(BF16)
    off_x = grad_copy(g_off.at[1], r_buf.at[0], 0, (r_off, c_x))
    off_far = grad_copy(g_off.at[2], r_buf.at[1], 1, (r_off, c_take))
    off_own = grad_copy(g_off.at[0], r_buf.at[2], 2, (r_off, c))
    across_grads = [off_x, off_own]
    pl.when(inside)(lambda: start([off_x]))
    for j in order:
        g_own[j] = dot(spread[:t], zbuf[j])
    sum_x = grad_copy(g_sum.at[0], r_buf.at[3], 3, (r, c_x))
    sum_far = grad_copy(g_sum.at[1], r_buf.at[4], 4, (r, c_take))
    for j in (1, 2):
        on_copies[j].wait_recv()
        g_sum[j - 1] = (g_own[j] + r_on_buf[j].astype(F32)).astype(BF16)
        if j == 1:
            sum_x.start()
    pl.when(takes)(lambda: start([sum_far]))
    pl.when(inside & takes)(lambda: start([off_far]))
    pl.when(inside)(lambda: start([off_own]))
    on_copies[0].wait_recv()
    mine = g_own[0] + r_on_buf[0].astype(F32)
    pl.when(inside)(lambda: wait_recv(across_grads))
    pl.when(inside & gives)(lambda: wait_recv([off_far]))
    pl.when(gives)(lambda: wait_recv([sum_far]))
    wait_recv([sum_x])
    for i in range(5):
        mine = mine + r_buf[i].astype(F32)
    out[0] = mine[:, :t]
    out[1] = mine[:, t:]
    wait_send(first + meas_x + [fwd_x, sum_x] + on_copies)
    pl.when(gives)(lambda: wait_send([to_far]))
    pl.when(takes)(lambda: wait_send([fwd_far, sum_far]))
    pl.when(inside & gives)(lambda: wait_send([to_off_far]))
    pl.when(inside & takes)(lambda: wait_send([off_far]))
    wait_send(meas_own + sum(meas_fwd, []))
    pl.when(inside)(lambda: wait_send(across_copies + across_grads))


def per_device(n_r, n_c, tables, specimen, probe, measured, centers, counts, helpers):
    t = specimen.shape[1]
    modes, _, n, _ = probe.shape
    fwd, bwd = tables
    vmem = pl.BlockSpec(memory_space=pltpu.VMEM)
    hbm = pl.BlockSpec(memory_space=pl.ANY)
    dma = pltpu.SemaphoreType.DMA
    return pl.pallas_call(
        functools.partial(kernel, n_r, n_c),
        out_shape=pltpu.VMEM(specimen.shape, F32),
        in_specs=[hbm] * 8,
        out_specs=vmem,
        scratch_shapes=[
            pltpu.VMEM(centers.shape, jnp.int32),
            pltpu.VMEM(counts.shape, jnp.int32),
            pltpu.VMEM(helpers.shape, jnp.int32),
            pltpu.VMEM(specimen.shape, F32),
            pltpu.VMEM((n, n), F32),
            pltpu.VMEM(probe.shape, F32),
            pltpu.VMEM((2 * n, 2 * n), BF16),
            pltpu.VMEM((2 * n, 2 * n), BF16),
            pltpu.VMEM((2, 8, 128), jnp.int32),
            pltpu.VMEM((9, t, 2 * t), BF16),
            pltpu.VMEM((n_c, CHUNKS, n // CHUNKS, n), BF16),
            pltpu.VMEM((2, modes * n, 2 * n), BF16),
            pltpu.VMEM((2, 2 * n, modes * n), BF16),
            pltpu.VMEM((2, 2 * n, modes * n), F32),
            pltpu.VMEM((2, 2 * n, modes * n), F32),
            pltpu.VMEM((3, 2 * n, 2 * t), BF16),
            pltpu.VMEM((3, t, 2 * t), F32),
            pltpu.VMEM((3, t, 2 * t), BF16),
            pltpu.VMEM((3, t, 2 * t), BF16),
            pltpu.VMEM((2, t, 2 * t), BF16),
            pltpu.VMEM((3, t, 2 * t), BF16),
            pltpu.VMEM((5, t, 2 * t), BF16),
            dma((8,)),
            dma((2,)),
            dma((9,)),
            dma((9,)),
            dma((CHUNKS + (CHUNKS + 1) * (n_c // 2 - 1),)),
            dma((CHUNKS + (CHUNKS + 1) * (n_c // 2 - 1),)),
            dma((8,)),
            dma((8,)),
        ],
        compiler_params=pltpu.CompilerParams(
            collective_id=0, has_side_effects=True, vmem_limit_bytes=56 * 1024 * 1024
        ),
    )(
        centers,
        counts,
        helpers,
        specimen,
        measured.reshape(n, n),
        probe,
        fwd,
        bwd,
    )


def solution(mesh):
    n_r, n_c = mesh.shape["row"], mesh.shape["col"]

    def program(specimen, probe, measured, centers, counts, helpers):
        base = dft_blocks(probe.shape[-1])
        tables = (jnp.asarray(base, BF16), jnp.asarray(base.T, BF16))
        return jax.shard_map(
            functools.partial(per_device, n_r, n_c, tables),
            mesh=mesh,
            in_specs=(
                P(None, "row", "col"),
                P(),
                P("row", "col", None, None, None),
                P("row", "col", None, None),
                P("row", "col"),
                P("row", "col", None),
            ),
            out_specs=P(None, "row", "col"),
            check_vma=False,
        )(specimen, probe, measured, centers, counts, helpers)

    return program
```

```python
import functools
import math

import jax
import jax.numpy as jnp
import numpy as np
from jax import lax
from jax.experimental import pallas as pl
from jax.experimental.pallas import tpu as pltpu
from jax.sharding import PartitionSpec as P

MESH = pl.DeviceIdType.MESH
F32 = jnp.float32
BF16 = jnp.bfloat16
CHUNKS = 4


def dft_blocks(extent):
    idx = np.arange(extent)
    angles = (idx[:, None] * idx[None, :] % extent) * (2.0 * math.pi / extent)
    scale = 1.0 / math.sqrt(extent)
    re, im = np.cos(angles) * scale, -np.sin(angles) * scale
    return np.block([[re, im], [-im, re]])


def dot(a, b):
    return jnp.dot(a, b, preferred_element_type=F32)


def kernel(
    n_r,
    n_c,
    centers_hbm,
    counts_hbm,
    helpers_hbm,
    spec_hbm,
    measured_hbm,
    probe_hbm,
    fwd_hbm,
    bwd_hbm,
    out,
    centers,
    counts,
    helpers,
    spec,
    measured,
    probe,
    fwd,
    bwd,
    meta,
    nb,
    meas,
    rows_buf,
    cols_buf,
    far,
    chi,
    zbuf,
    g_own,
    g_on,
    g_off,
    g_sum,
    r_on_buf,
    r_buf,
    local_sem,
    meta_sem,
    halo_send,
    halo_recv,
    meas_send,
    meas_recv,
    grad_send,
    grad_recv,
):
    t = spec.shape[1]
    n = probe.shape[-1]
    modes = probe.shape[0]
    r, c = lax.axis_index("row"), lax.axis_index("col")
    odd_r, odd_c = lax.rem(r, 2), lax.rem(c, 2)
    r_on = r + 1 - 2 * odd_r
    r_off = lax.rem(r - 1 + 2 * odd_r + n_r, n_r)
    inside = (r > 0) & (r < n_r - 1)
    gives = (c > 0) & (c < n_c - 1)
    takes = (c != 1) & (c != n_c - 2)
    c_x = c + 1 - 2 * odd_c
    c_give = lax.rem(c - 2 + 4 * odd_c + n_c, n_c)
    c_take = lax.rem(c + 2 - 4 * odd_c + n_c, n_c)
    peers = [lax.rem(c + 2 * k, n_c) for k in range(1, n_c // 2)]

    barrier = pltpu.get_barrier_semaphore()
    near = [(r_on, c), (r, c_x)] + [(r, p) for p in peers]
    across = [(r_off, c), (r_off, c_x)]

    def greet(partners):
        for partner in partners:
            pl.semaphore_signal(barrier, inc=1, device_id=partner, device_id_type=MESH)

    greet(near)
    pl.when(inside)(lambda: greet(across))
    pl.when(inside & gives)(lambda: greet([(r_off, c_give)]))
    pl.when(inside & takes)(lambda: greet([(r_off, c_take)]))

    loads = [
        pltpu.make_async_copy(src, dst, local_sem.at[i])
        for i, (src, dst) in enumerate(
            [
                (spec_hbm, spec),
                (centers_hbm, centers),
                (counts_hbm, counts),
                (helpers_hbm, helpers),
                (measured_hbm, measured),
                (probe_hbm, probe),
                (fwd_hbm, fwd),
                (bwd_hbm, bwd),
            ]
        )
    ]
    for load in loads:
        load.start()

    loads[0].wait()
    nb[0] = jnp.concatenate([spec[0], spec[1]], axis=1).astype(BF16)
    for load in loads[1:4]:
        load.wait()
    at, to = centers[0, 0], helpers[0]
    values = [at[i : i + 1, j : j + 1] for i in range(2) for j in range(2)]
    values += [to[:, 0:1], to[:, 1:2], counts[...]]
    which = lax.broadcasted_iota(jnp.int32, (8, 128), 0)
    block = jnp.zeros((8, 128), jnp.int32)
    for i, value in enumerate(values):
        block = jnp.where(which == i, value, block)
    meta[0] = block
    loads[4].wait()
    meas[c] = measured[...].astype(BF16).reshape(meas.shape[1:])

    @pl.when(jnp.logical_not(inside))
    def _():
        nb[6:9] = jnp.zeros((3, t, 2 * t), BF16)
        r_buf[0:3] = jnp.zeros((3, t, 2 * t), BF16)

    @pl.when(jnp.logical_not(takes))
    def _():
        for i in (2, 5, 8):
            nb[i] = jnp.zeros((t, 2 * t), BF16)

    @pl.when(jnp.logical_not(gives))
    def _():
        for i in (1, 4):
            r_buf[i] = jnp.zeros((t, 2 * t), BF16)

    over = len(across) + jnp.where(gives, 1, 0) + jnp.where(takes, 1, 0)
    pl.semaphore_wait(barrier, len(near) + jnp.where(inside, over, 0))

    def remote(src, dst, send, recv, device):
        return pltpu.make_async_remote_copy(
            src_ref=src,
            dst_ref=dst,
            send_sem=send,
            recv_sem=recv,
            device_id=device,
            device_id_type=MESH,
        )

    def halo(src, dst, device):
        return remote(nb.at[src], nb.at[dst], halo_send.at[dst], halo_recv.at[dst], device)

    to_x = halo(0, 1, (r, c_x))
    to_off_x = halo(0, 7, (r_off, c_x))
    to_far = halo(0, 2, (r, c_give))
    to_off_far = halo(0, 8, (r_off, c_give))
    to_off = halo(0, 6, (r_off, c))
    to_on = halo(0, 3, (r_on, c))
    meta_copy = remote(meta.at[0], meta.at[1], meta_sem.at[0], meta_sem.at[1], (r, c_x))
    first = [meta_copy, to_x, to_on]
    across_copies = [to_off_x, to_off]

    def start(copies):
        for copy in copies:
            copy.start()

    def wait_recv(copies):
        for copy in copies:
            copy.wait_recv()

    def wait_send(copies):
        for copy in copies:
            copy.wait_send()

    start(first[:2])
    pl.when(inside)(lambda: start(across_copies))
    pl.when(inside & gives)(lambda: start([to_off_far]))
    pl.when(gives)(lambda: start([to_far]))
    start(first[2:])

    chunks = meas.shape[1]
    sides = n_c // 2 - 1

    def meas_copy(src, sem, device):
        return remote(src, src, meas_send.at[sem], meas_recv.at[sem], device)

    meas_x = [meas_copy(meas.at[c, q], q, (r, c_x)) for q in range(chunks)]
    meas_own = [meas_copy(meas.at[c], chunks + k, (r, p)) for k, p in enumerate(peers)]
    meas_fwd = [
        [
            meas_copy(meas.at[c_x, q], chunks + sides * (q + 1) + k, (r, p))
            for k, p in enumerate(peers)
        ]
        for q in range(chunks)
    ]
    start(meas_x)
    start(meas_own)

    def pass_on(some):
        for q in some:
            meas_x[q].wait_recv()
            start(meas_fwd[q])

    to_x.wait_recv()
    fwd_x = halo(1, 4, (r_on, c))
    fwd_x.start()
    fwd_far = halo(2, 5, (r_on, c))

    @pl.when(takes)
    def _():
        to_far.wait_recv()
        fwd_far.start()


    meta_copy.wait_recv()
    info = meta[1]
    cr = [info[0:1, 0:1], info[2:3, 0:1]]
    cc = [info[1:2, 0:1], info[3:4, 0:1]]
    hc = [info[4:5, 0:1], info[5:6, 0:1]]
    live = [info[6:7, 0:1] > s for s in range(2)]

    nowhere = -4 * n
    row_on, row_off = 2 * t * (1 - odd_r), 2 * t * odd_r
    row_off = jnp.where((r == 0) | (r == n_r - 1), nowhere, row_off)
    col_own, col_far = 2 * t * odd_c, 2 * t * (1 - odd_c)
    col_far = jnp.where((c == 1) | (c == n_c - 2), nowhere, col_far)

    def place(idx, first_, second, third):
        role = idx // t
        base = jnp.where(role == 0, first_, jnp.where(role == 1, second, third))
        return base + idx - role * t

    def one_hot(shape, axis, roles, start):
        role_idx = lax.broadcasted_iota(jnp.int32, shape, axis)
        pix = lax.broadcasted_iota(jnp.int32, shape, 1 - axis)
        return jnp.where(place(role_idx, *roles) == pix + start, 1.0, 0.0).astype(BF16)

    row_roles = (t, row_on, row_off)
    col_roles = (col_own, t, col_far)
    row_at = [jnp.where(live[s], cr[s], 8 * n) for s in range(2)]

    pl.when(inside)(lambda: wait_recv(across_copies))
    pl.when(inside & takes)(lambda: wait_recv([to_off_far]))
    pl.when(takes)(lambda: wait_recv([fwd_far]))
    wait_recv([to_on, fwd_x])
    for load in loads[5:]:
        load.wait()

    tiles = [jnp.concatenate([nb[j], nb[3 + j], nb[6 + j]], axis=0) for j in range(3)]

    for s in range(2):
        pick = one_hot((n, 3 * t), 1, row_roles, row_at[s])
        cut = [dot(pick, tiles[j]).astype(BF16) for j in range(3)]
        strip = jnp.concatenate(
            [
                jnp.concatenate([x[:, :t] for x in cut], axis=1),
                jnp.concatenate([x[:, t:] for x in cut], axis=1),
            ],
            axis=0,
        )
        patch = dot(strip, one_hot((3 * t, n), 0, col_roles, cc[s]))
        re, im = patch[:n], patch[n:]
        for k in range(modes):
            p_re, p_im = probe[k, 0], probe[k, 1]
            rows_buf[s, k * n : (k + 1) * n, :n] = (p_re * re - p_im * im).astype(BF16)
            rows_buf[s, k * n : (k + 1) * n, n:] = (p_re * im + p_im * re).astype(BF16)
        for k in range(modes):
            half = dot(rows_buf[s, k * n : (k + 1) * n], fwd[...]).astype(BF16)
            cols_buf[s, :n, k * n : (k + 1) * n] = half[:, :n]
            cols_buf[s, n:, k * n : (k + 1) * n] = half[:, n:]
        far[s] = dot(bwd[...], cols_buf[s])
        pass_on(range(s * chunks // 2, (s + 1) * chunks // 2))

    w = n // chunks
    halves = [
        jnp.concatenate([fwd[:, i * t : (i + 1) * t], fwd[:, n + i * t : n + (i + 1) * t]], axis=1)
        for i in range(2)
    ]
    wait_recv(meas_own)
    for q in range(chunks):
        wait_recv(meas_fwd[q])
        lo, block = q * w, modes * w
        for s in range(2):
            intensity = jnp.zeros((w, n), F32)
            for k in range(modes):
                f_re = far[s, lo : lo + w, k * n : (k + 1) * n]
                f_im = far[s, n + lo : n + lo + w, k * n : (k + 1) * n]
                intensity = intensity + (f_re * f_re + f_im * f_im)
            amp = jnp.zeros((w, n), F32)
            for h in range(n_c):
                amp = amp + jnp.where(hc[s] == h, meas[h, q].astype(F32), 0.0)
            factor = 1.0 - amp * lax.rsqrt(jnp.maximum(intensity, 0.25))
            for k in range(modes):
                at = q * block + k * w
                for part in range(2):
                    row = part * n + lo
                    f = far[s, row : row + w, k * n : (k + 1) * n]
                    rows_buf[s, at : at + w, part * n : (part + 1) * n] = (f * factor).astype(BF16)
            back = dot(rows_buf[s, q * block : (q + 1) * block], bwd[...]).astype(BF16)
            for k in range(modes):
                for part in range(2):
                    row = lo // t * n + part * t + lo % t
                    cols_buf[s, row : row + w, k * n : (k + 1) * n] = back[
                        k * w : (k + 1) * w, part * n : (part + 1) * n
                    ]

        if q == chunks // 2 - 1:
            for s in range(2):
                chi[s] = dot(halves[0], cols_buf[s, :n])

    for s in range(2):
        chi[s] = chi[s] + dot(halves[1], cols_buf[s, n:])
        g_re = jnp.zeros((n, n), F32)
        g_im = jnp.zeros((n, n), F32)
        for k in range(modes):
            p_re, p_im = probe[k, 0], probe[k, 1]
            x_re = chi[s, :n, k * n : (k + 1) * n]
            x_im = chi[s, n:, k * n : (k + 1) * n]
            g_re = g_re + (p_re * x_re + p_im * x_im)
            g_im = g_im + (p_re * x_im - p_im * x_re)
        grad = jnp.concatenate([g_re, g_im], axis=0).astype(BF16)
        wide = dot(grad, one_hot((n, 3 * t), 1, col_roles, cc[s])).astype(BF16)
        for j in range(3):
            zbuf[j, s * n : (s + 1) * n, :t] = wide[:n, j * t : (j + 1) * t]
            zbuf[j, s * n : (s + 1) * n, t:] = wide[n:, j * t : (j + 1) * t]

    spread = jnp.concatenate(
        [one_hot((3 * t, n), 0, row_roles, row_at[s]) for s in range(2)], axis=1
    )

    def grad_copy(src, dst, i, device):
        return remote(src, dst, grad_send.at[i], grad_recv.at[i], device)

    order = (1, 2, 0)
    on_copies = [grad_copy(g_on.at[j], r_on_buf.at[j], 5 + j, (r_on, c)) for j in range(3)]
    off_x = grad_copy(g_off.at[1], r_buf.at[0], 0, (r_off, c_x))
    off_far = grad_copy(g_off.at[2], r_buf.at[1], 1, (r_off, c_take))
    off_own = grad_copy(g_off.at[0], r_buf.at[2], 2, (r_off, c))
    across_grads = [off_x, off_own]
    g_on[1] = dot(spread[t : 2 * t], zbuf[1]).astype(BF16)
    on_copies[1].start()
    g_off[1] = dot(spread[2 * t :], zbuf[1]).astype(BF16)
    pl.when(inside)(lambda: start([off_x]))
    for j in order[1:]:
        g_on[j] = dot(spread[t : 2 * t], zbuf[j]).astype(BF16)
        on_copies[j].start()
    for j in order:
        g_own[j] = dot(spread[:t], zbuf[j])
    sum_x = grad_copy(g_sum.at[0], r_buf.at[3], 3, (r, c_x))
    sum_far = grad_copy(g_sum.at[1], r_buf.at[4], 4, (r, c_take))
    for j in (1, 2):
        on_copies[j].wait_recv()
        g_sum[j - 1] = (g_own[j] + r_on_buf[j].astype(F32)).astype(BF16)
        if j == 1:
            sum_x.start()
            for i in order[1:]:
                g_off[i] = dot(spread[2 * t :], zbuf[i]).astype(BF16)
    pl.when(takes)(lambda: start([sum_far]))
    pl.when(inside & takes)(lambda: start([off_far]))
    pl.when(inside)(lambda: start([off_own]))
    on_copies[0].wait_recv()
    mine = g_own[0] + r_on_buf[0].astype(F32)
    pl.when(inside)(lambda: wait_recv(across_grads))
    pl.when(inside & gives)(lambda: wait_recv([off_far]))
    pl.when(gives)(lambda: wait_recv([sum_far]))
    wait_recv([sum_x])
    for i in range(5):
        mine = mine + r_buf[i].astype(F32)
    out[0] = mine[:, :t]
    out[1] = mine[:, t:]
    wait_send(first + meas_x + [fwd_x, sum_x] + on_copies)
    pl.when(gives)(lambda: wait_send([to_far]))
    pl.when(takes)(lambda: wait_send([fwd_far, sum_far]))
    pl.when(inside & gives)(lambda: wait_send([to_off_far]))
    pl.when(inside & takes)(lambda: wait_send([off_far]))
    wait_send(meas_own + sum(meas_fwd, []))
    pl.when(inside)(lambda: wait_send(across_copies + across_grads))


def per_device(n_r, n_c, tables, specimen, probe, measured, centers, counts, helpers):
    t = specimen.shape[1]
    modes, _, n, _ = probe.shape
    fwd, bwd = tables
    vmem = pl.BlockSpec(memory_space=pltpu.VMEM)
    hbm = pl.BlockSpec(memory_space=pl.ANY)
    dma = pltpu.SemaphoreType.DMA
    return pl.pallas_call(
        functools.partial(kernel, n_r, n_c),
        out_shape=pltpu.VMEM(specimen.shape, F32),
        in_specs=[hbm] * 8,
        out_specs=vmem,
        scratch_shapes=[
            pltpu.VMEM(centers.shape, jnp.int32),
            pltpu.VMEM(counts.shape, jnp.int32),
            pltpu.VMEM(helpers.shape, jnp.int32),
            pltpu.VMEM(specimen.shape, F32),
            pltpu.VMEM((n, n), F32),
            pltpu.VMEM(probe.shape, F32),
            pltpu.VMEM((2 * n, 2 * n), BF16),
            pltpu.VMEM((2 * n, 2 * n), BF16),
            pltpu.VMEM((2, 8, 128), jnp.int32),
            pltpu.VMEM((9, t, 2 * t), BF16),
            pltpu.VMEM((n_c, CHUNKS, n // CHUNKS, n), BF16),
            pltpu.VMEM((2, modes * n, 2 * n), BF16),
            pltpu.VMEM((2, 2 * n, modes * n), BF16),
            pltpu.VMEM((2, 2 * n, modes * n), F32),
            pltpu.VMEM((2, 2 * n, modes * n), F32),
            pltpu.VMEM((3, 2 * n, 2 * t), BF16),
            pltpu.VMEM((3, t, 2 * t), F32),
            pltpu.VMEM((3, t, 2 * t), BF16),
            pltpu.VMEM((3, t, 2 * t), BF16),
            pltpu.VMEM((2, t, 2 * t), BF16),
            pltpu.VMEM((3, t, 2 * t), BF16),
            pltpu.VMEM((5, t, 2 * t), BF16),
            dma((8,)),
            dma((2,)),
            dma((9,)),
            dma((9,)),
            dma((CHUNKS + (CHUNKS + 1) * (n_c // 2 - 1),)),
            dma((CHUNKS + (CHUNKS + 1) * (n_c // 2 - 1),)),
            dma((8,)),
            dma((8,)),
        ],
        compiler_params=pltpu.CompilerParams(
            collective_id=0, has_side_effects=True, vmem_limit_bytes=56 * 1024 * 1024
        ),
    )(
        centers,
        counts,
        helpers,
        specimen,
        measured.reshape(n, n),
        probe,
        fwd,
        bwd,
    )


def solution(mesh):
    n_r, n_c = mesh.shape["row"], mesh.shape["col"]

    def program(specimen, probe, measured, centers, counts, helpers):
        base = dft_blocks(probe.shape[-1])
        tables = (jnp.asarray(base, BF16), jnp.asarray(base.T, BF16))
        return jax.shard_map(
            functools.partial(per_device, n_r, n_c, tables),
            mesh=mesh,
            in_specs=(
                P(None, "row", "col"),
                P(),
                P("row", "col", None, None, None),
                P("row", "col", None, None),
                P("row", "col"),
                P("row", "col", None),
            ),
            out_specs=P(None, "row", "col"),
            check_vma=False,
        )(specimen, probe, measured, centers, counts, helpers)

    return program
```
